32 devices in a mesh: ctx: 4 (over y, core), seq: 4 (over z), tp: 2 (over x).
Axes of the slice: x: 2, y: 2, z: 4, core: 2. Of those that a mesh axis runs over, the one named last changes fastest.
Arguments:
- inputs: bfloat16 [4, 512, 4096], P('seq', 'ctx', 'tp'), may hold values from -6 to 6
- gating: bfloat16 [4, 512, 4096], P('seq', 'ctx', 'tp'), may hold values from -6 to 6
- write_proj: bfloat16 [4, 512, 8, 128], P('seq', 'ctx', 'tp'), may hold values from -6 to 6
- read_proj: bfloat16 [4, 512, 8, 128], P('seq', 'ctx', 'tp'), may hold values from -0.5390625 to 0.5390625
- step_raw: float32 [4, 512, 64], P('seq', 'ctx', 'tp'), may hold values from -2 to 256
- decay_log: float32 [64], P('tp'), may hold values from -11 to -3
- skip_gain: float32 [64], P('tp'), may hold values from 0.5 to 2
- norm_gain: float32 [4096], P('tp'), may hold values from 0.5 to 1.5
- out_weight: bfloat16 [4096, 2048], P('tp', 'ctx'), may hold values from -0.09375 to 0.09375
- residual: bfloat16 [4, 512, 2048], P('seq', 'ctx', 'tp'), may hold values from -32 to 32
- routes: int32 [4, 512, 2], P('seq', 'ctx'), may hold values from 0 to 7, all different within a row; in each aligned block of 128 rows (0 to 127, 128 to 255, ..., all dimensions but the last counted through in order) at most 48 rows name the same one
- route_weight: float32 [4, 512, 2], P('seq', 'ctx'), may hold values from 0.2 to 1
- layer_gain: float32 [2048], P('tp'), may hold values from 0.5 to 1.5
- gate_up_codes: bfloat16 [16, 2, 2048, 768], P(('ctx', 'seq'), None, 'tp'), may hold values from -0.125 to 0.125
- gate_up_scales: float32 [16, 2, 16, 6], P(('ctx', 'seq'), None, 'tp'), may hold values from 0.5 to 2
- down_codes: bfloat16 [16, 768, 2048], P(('ctx', 'seq'), None, 'tp'), may hold values from -0.15625 to 0.15625
- down_scales: float32 [16, 6, 16], P(('ctx', 'seq'), None, 'tp'), may hold values from 0.5 to 2
Outputs:
- mixed: bfloat16 [4, 512, 2048], P('seq', 'ctx', 'tp')
The draws below stay inside these ranges and needn't reach their ends.
Inputs may be any that keep to these rules, and one draw needn't show every extreme that they name: `routes`: each row names 2 different experts. In each aligned block of 128 rows (the positions of one sequence on one device) no expert is named by more than 48 rows, a bound that some block reaches.
All inputs are finite; a program needn't handle non-finite values.
Results may differ from the reference program's by a relative error of at most 0.033.
Values may be sent and summed in bfloat16 or wider, within the bound.
A program may use at most 64 MiB of HBM per device.

```python
import math
import jax
import jax.numpy as jnp
import numpy as np
from jax import lax

D = 2048
HEADS = 64
P_SIZE = 64
NST = 128
NGROUPS = 8
QLEN = 128
QB = 128
HID = 1536
TOPK = 2
TOK_DEV = 128
NSEQ = 4
LEN = 512
INNER = 4096
HALF = 768
EXPERTS = 8
CAP = 48
N_TP = 2


def draw_step_raw(key, part):
    key_block, key_token, key_place, key_height = jax.random.split(key, 4)
    blocks = LEN // TOK_DEV
    block_rate = jnp.exp(jax.random.uniform(key_block, (NSEQ, blocks, 1, 1), jnp.float32, math.log(0.5), math.log(2.0)))
    token_rate = jax.random.uniform(key_token, (NSEQ, blocks, TOK_DEV, HEADS), jnp.float32, 0.5, 1.5)
    stride_size = (block_rate * token_rate).reshape(NSEQ, LEN, HEADS)
    places = jax.random.randint(key_place, (NSEQ, 2), 0, LEN)
    segment_span = jax.random.uniform(key_height, (NSEQ, 2), jnp.float32, 0.3, 0.5) * LEN
    hidden_future_cells = jnp.arange(LEN)[None, :, None] == places[:, None, :]
    word_groupings = jnp.sum(jnp.where(hidden_future_cells, segment_span[:, None, :], 0.0), axis=-1)
    stride_size = jnp.where(word_groupings[:, :, None] > 0.0, word_groupings[:, :, None], stride_size)
    return stride_size + jnp.log(-jnp.expm1(-stride_size))


def draw_decay_log(key, part):
    key_kind, key_fast, key_slow = jax.random.split(key, 3)
    quick = jax.random.randint(key_kind, (HEADS,), 0, 10) < 5
    fast_rate = jax.random.uniform(key_fast, (HEADS,), jnp.float32, math.log(1.0 / 50.0), math.log(1.0 / 30.0))
    slow_rate = jnp.log(jax.random.uniform(key_slow, (HEADS,), jnp.float32, 0.6, 1.0) / LEN)
    return jnp.where(quick, fast_rate, slow_rate)


def draw_residual(key, part):
    key_rows, key_cols, key_base = jax.random.split(key, 3)
    row_scale = jnp.exp(jax.random.uniform(key_rows, (NSEQ, LEN, 1), jnp.float32, math.log(0.2), math.log(2.0)))
    column_scale_factor = 3.0 ** (jnp.arange(D, dtype=jnp.float32) / D) * jnp.exp(jax.random.uniform(key_cols, (D,), jnp.float32, math.log(0.3), 0.0))
    base = jax.random.truncated_normal(key_base, -4.0, 4.0, (NSEQ, LEN, D), jnp.float32)
    return (base * row_scale * column_scale_factor).astype(jnp.bfloat16)


def steps_of(key, dims, cuts, smallest, largest):
    gain, own = 1.0, jax.random.fold_in(key, 6)
    for axis_at, shards_of in cuts:
        heights = jnp.exp(jax.random.uniform(jax.random.fold_in(own, axis_at), (shards_of,), jnp.float32, smallest / len(cuts), largest / len(cuts)))
        gain = gain * jnp.repeat(heights, dims[axis_at] // shards_of).reshape([-1 if axis == axis_at else 1 for axis in range(len(dims))])
    return gain


def assign_block(stream_key, own, number, rows, number_of, top, most, slope):
    sequence = jax.random.permutation(stream_key, number_of)
    crowded, usual = portions_of(number_of, rows * top, most, slope, True), portions_of(number_of, rows * top, most, slope, False)
    places = jnp.arange(number_of)

    def named(lengths, turn):
        used = int((lengths > 0).sum())
        fixed = max(1, used // 4)
        shifted = fixed + (places - fixed + turn * (used - fixed)) % max(1, number_of - fixed)
        return jnp.zeros((number_of,), jnp.int32).at[sequence[jnp.where(places < fixed, places, shifted)]].set(jnp.asarray(lengths, jnp.int32))

    lengths = jnp.where(number % 4 == 0, named(crowded, number // 4), named(usual, number - number // 4 - 1))
    mixed = jax.random.permutation(jax.random.fold_in(own, 3), number_of)
    donor, sink = mixed[0:number_of // 2 * 2:2], mixed[1:number_of // 2 * 2:2]
    slack = jnp.minimum(lengths[donor] - 1, most - lengths[sink]) // 2
    slack = jnp.where((donor == sequence[0]) | (sink == sequence[0]) | (lengths[sink] == 0), 0, jnp.maximum(slack, 0))
    shifted = jax.random.randint(jax.random.fold_in(own, 4), (number_of // 2,), 0, 1 << 20) % (slack + 1)
    lengths = lengths.at[donor].add(-shifted).at[sink].add(shifted)
    labels = jnp.searchsorted(jnp.cumsum(lengths), jnp.arange(rows * top), side="right").astype(jnp.int32)
    table = labels.reshape(top, rows).T
    table = table[jax.random.permutation(jax.random.fold_in(own, 1), rows)]
    turn = jax.random.randint(jax.random.fold_in(own, 2), (rows, 1), 0, top)
    return jnp.take_along_axis(table, (jnp.arange(top)[None, :] + turn) % top, axis=1)


def portions_of(count, total, most, lean, full):
    weights = [(1 << 20) // math.isqrt(rank ** lean) + 1 for rank in range(1, count + 1)]
    largest = most if full else min(most, max(-(-total // count), total * weights[0] // sum(weights)))
    least = 1 if total - largest >= count - 1 else 0
    holding, surplus = [largest] + [least] * (count - 1), total - largest - least * (count - 1)
    while surplus > 0:
        movable = [i for i in range(1, count) if holding[i] < largest] or [i for i in range(1, count) if holding[i] < most]
        pool, remaining = sum([weights[i] for i in movable]), surplus
        for i in movable:
            addition = min(most - holding[i], max(1, remaining * weights[i] // pool), surplus)
            holding[i] = holding[i] + addition
            surplus = surplus - addition
    return np.array(holding)


def gaussian(own_key, dims, scale, limit, shards=(), kind=jnp.bfloat16):
    drawn = jax.random.normal(own_key, dims, jnp.float32) * scale
    if len(shards) > 0:
        drawn = steps_of(own_key, dims, shards, -0.22, 0.18) * drawn
    return jnp.clip(drawn, min=-limit, max=limit).astype(kind)


def setup_inputs(seed: int = 0) -> dict:
    streams_of = jax.random.split(jax.random.key(seed), 18)
    inputs = gaussian(streams_of[0], (NSEQ, LEN, INNER), 1.0, 6.0, ((0, 4), (1, 4), (2, 2)))
    gating = gaussian(streams_of[1], (NSEQ, LEN, INNER), 1.0, 6.0, ((0, 4), (1, 4), (2, 2)))
    write_proj = gaussian(streams_of[2], (NSEQ, LEN, NGROUPS, NST), 1.0, 6.0, ((0, 4), (1, 4), (2, 2)))
    read_proj = gaussian(streams_of[3], (NSEQ, LEN, NGROUPS, NST), 0.09, 0.5390625, ((0, 4), (1, 4), (2, 2)))
    step_raw = draw_step_raw(jax.random.fold_in(streams_of[17], 71), 0)
    decay_log = draw_decay_log(jax.random.fold_in(streams_of[17], 71), 0)
    skip_gain = jnp.clip(0.5 + 1.5 * jax.random.uniform(streams_of[6], (HEADS,), jnp.float32) ** steps_of(streams_of[6], (HEADS,), ((0, 2),), -0.2, 0.2), 0.5, 2.0)
    norm_gain = jnp.clip(1.0 + 0.1 * jax.random.normal(streams_of[7], (INNER,), jnp.float32), 0.5, 1.5)
    out_weight = gaussian(streams_of[8], (INNER, D), INNER ** -0.5, 0.09375, ((0, 2), (1, 4)))
    residual = draw_residual(jax.random.fold_in(streams_of[17], 71), 0)
    routes_keys = jax.random.split(jax.random.fold_in(streams_of[10], 1), NSEQ * LEN // TOK_DEV)
    routes_turns = jax.random.permutation(jax.random.fold_in(streams_of[10], 3), NSEQ * LEN // TOK_DEV)
    routes = jax.vmap(lambda own, number: assign_block(jax.random.fold_in(streams_of[10], 2), own, number, TOK_DEV, EXPERTS, TOPK, CAP, 2))(routes_keys, routes_turns).reshape((NSEQ, LEN, TOPK))
    route_weight = jnp.clip(0.2 + 0.8 * jax.random.uniform(streams_of[11], (NSEQ, LEN, TOPK), jnp.float32) ** steps_of(streams_of[11], (NSEQ, LEN, TOPK), ((0, 4), (1, 4)), -0.2, 0.2), 0.2, 1.0)
    layer_gain = jnp.clip(1.0 + 0.1 * jax.random.normal(streams_of[12], (D,), jnp.float32), 0.5, 1.5)
    gate_up_codes = gaussian(streams_of[13], (2 * EXPERTS, 2, D, HALF), D ** -0.5, 0.125, ((0, 16), (2, 2)))
    gate_up_scales = jnp.clip(jnp.exp(math.log(2.0) - 1.3862944 * jax.random.uniform(streams_of[14], (2 * EXPERTS, 2, D // QB, HALF // QB), jnp.float32) ** steps_of(streams_of[14], (2 * EXPERTS, 2, D // QB, HALF // QB), ((0, 16), (2, 2)), -0.2, 0.2)), 0.5, 2.0)
    down_codes = gaussian(streams_of[15], (2 * EXPERTS, HALF, D), HID ** -0.5, 0.15625, ((0, 16), (2, 2)))
    down_scales = jnp.clip(jnp.exp(math.log(2.0) - 1.3862944 * jax.random.uniform(streams_of[16], (2 * EXPERTS, HALF // QB, D // QB), jnp.float32) ** steps_of(streams_of[16], (2 * EXPERTS, HALF // QB, D // QB), ((0, 16), (2, 2)), -0.2, 0.2)), 0.5, 2.0)
    return {"inputs": inputs, "gating": gating, "write_proj": write_proj, "read_proj": read_proj, "step_raw": step_raw, "decay_log": decay_log, "skip_gain": skip_gain, "norm_gain": norm_gain, "out_weight": out_weight, "residual": residual, "routes": routes, "route_weight": route_weight, "layer_gain": layer_gain, "gate_up_codes": gate_up_codes, "gate_up_scales": gate_up_scales, "down_codes": down_codes, "down_scales": down_scales}


EPSILON = 1e-05

def expand_scales(scales, width):
    return jnp.repeat(jnp.repeat(scales, width, axis=-2), width, axis=-1)

def blender_series(pieces, decay_log, skip_gain, norm_gain, out_weight):
    inputs, gating, write_proj, read_proj, step_raw, residual = pieces
    blocks = LEN // QLEN
    per_group = HEADS // NGROUPS
    stride_size = jax.nn.softplus(step_raw)
    rate = -jnp.exp(decay_log)
    cumul = jnp.cumsum((stride_size * rate[None, :]).reshape(blocks, QLEN, HEADS), axis=1)
    values = inputs.reshape(blocks, QLEN, HEADS, P_SIZE)
    writes = write_proj.reshape(blocks, QLEN, NGROUPS, NST)
    reads = read_proj.reshape(blocks, QLEN, NGROUPS, NST)
    steps_block = stride_size.reshape(blocks, QLEN, HEADS)
    causal_mask = jnp.arange(QLEN)[:, None] >= jnp.arange(QLEN)[None, :]

    def advance(state, blockwise):
        value_blk, write_blk, read_blk, step_blk, cum_blk = blockwise
        scores = jnp.einsum('tgn,sgn->gts', read_blk.astype(jnp.float32), write_blk.astype(jnp.float32))
        scores = jnp.repeat(scores, per_group, axis=0)
        cum_heads = cum_blk.T
        spread = cum_heads[:, :, None] - cum_heads[:, None, :]
        decay = jnp.where(causal_mask, jnp.exp(jnp.where(causal_mask, spread, 0.0)), 0.0) * step_blk.T[:, None, :]
        mixing = (scores * decay).astype(jnp.bfloat16)
        local = jnp.einsum('hts,shp->thp', mixing.astype(jnp.float32), value_blk.astype(jnp.float32))
        final = cum_blk[-1]
        coefficient_array = jnp.exp(final[None, :] - cum_blk) * step_blk
        weighted = (value_blk.astype(jnp.float32) * coefficient_array[:, :, None]).astype(jnp.bfloat16)
        write_heads = jnp.repeat(write_blk, per_group, axis=1).astype(jnp.float32)
        read_heads = jnp.repeat(read_blk, per_group, axis=1).astype(jnp.float32)
        contrib = jnp.einsum('shp,shn->hpn', weighted.astype(jnp.float32), write_heads)
        carried = jnp.einsum('hpn,thn->thp', state, read_heads, precision=lax.Precision.HIGHEST)
        output = local + jnp.exp(cum_blk)[:, :, None] * carried + skip_gain[None, :, None] * value_blk.astype(jnp.float32)
        fresh = jnp.exp(final)[:, None, None] * state + contrib
        return (fresh, output)
    start = jnp.zeros((HEADS, P_SIZE, NST), jnp.float32)
    ending, outputs = lax.scan(advance, start, (values, writes, reads, steps_block, cumul))
    gated = outputs.reshape(LEN, INNER) * jax.nn.silu(gating.astype(jnp.float32))
    grouped = gated.reshape(LEN, NGROUPS, INNER // NGROUPS)
    normed = (grouped * lax.rsqrt(lax.optimization_barrier(jnp.mean(grouped * grouped, axis=-1, keepdims=True)) + EPSILON)).reshape(LEN, INNER)
    normed = (normed * norm_gain).astype(jnp.bfloat16)
    mixer = jnp.dot(normed, out_weight, preferred_element_type=jnp.float32)
    return (residual.astype(jnp.float32) + mixer).astype(jnp.bfloat16)

def rounded(value):
    return lax.optimization_barrier(value.astype(jnp.bfloat16)).astype(jnp.float32)

def reference(inputs, gating, write_proj, read_proj, step_raw, decay_log, skip_gain, norm_gain, out_weight, residual, routes, route_weight, layer_gain, gate_up_codes, gate_up_scales, down_codes, down_scales):
    stream = lax.map(lambda pieces: blender_series(pieces, decay_log, skip_gain, norm_gain, out_weight), (inputs, gating, write_proj, read_proj, step_raw, residual))
    wide = stream.astype(jnp.float32)
    expert_in = (wide * lax.rsqrt(lax.optimization_barrier(jnp.mean(wide * wide, axis=-1, keepdims=True)) + EPSILON) * layer_gain).astype(jnp.bfloat16)
    count = NSEQ * LEN
    flat_in = jnp.concatenate([expert_in.reshape(count, D), jnp.zeros((1, D), jnp.bfloat16)], axis=0)
    chosen = routes.reshape(count * TOPK).astype(jnp.int32)
    blocks = count // TOK_DEV
    block_of = (jnp.arange(count * TOPK) // (TOPK * TOK_DEV)).astype(jnp.int32)
    onehot = (chosen[:, None] == jnp.arange(EXPERTS)[None, :]).astype(jnp.int32).reshape(blocks, TOPK * TOK_DEV, EXPERTS)
    before = (jnp.cumsum(onehot, axis=1) - onehot).reshape(count * TOPK, EXPERTS)
    slot = jnp.take_along_axis(before, chosen[:, None], axis=1)[:, 0].astype(jnp.int32)
    token_ids = (jnp.arange(count * TOPK) // TOPK).astype(jnp.int32)
    token_of = jnp.full((EXPERTS, blocks, CAP), count, jnp.int32).at[chosen, block_of, slot].set(token_ids)
    weight_of = jnp.zeros((EXPERTS, blocks, CAP), jnp.float32).at[chosen, block_of, slot].set(route_weight.reshape(-1))
    fourth_portion = D // N_TP

    def per_expert(total, expert):
        flat_index = token_of[expert].reshape(-1)
        token_rows = flat_in[flat_index]
        summed = jnp.zeros((token_rows.shape[0], D), jnp.float32)
        for half in range(2):
            index = 2 * expert + half
            both = (gate_up_codes[index].astype(jnp.float32) * expand_scales(gate_up_scales[index], QB)).astype(jnp.bfloat16)
            down = (down_codes[index].astype(jnp.float32) * expand_scales(down_scales[index], QB)).astype(jnp.bfloat16)
            gate_sum = jnp.zeros((token_rows.shape[0], HALF), jnp.float32)
            up_sum = jnp.zeros((token_rows.shape[0], HALF), jnp.float32)
            for part_index in range(N_TP):
                portion = token_rows[:, part_index * fourth_portion:(part_index + 1) * fourth_portion]
                gate_sum = gate_sum + rounded(jnp.dot(portion, both[0, part_index * fourth_portion:(part_index + 1) * fourth_portion], preferred_element_type=jnp.float32))
                up_sum = up_sum + rounded(jnp.dot(portion, both[1, part_index * fourth_portion:(part_index + 1) * fourth_portion], preferred_element_type=jnp.float32))
            hidden = (jax.nn.silu(gate_sum) * up_sum).astype(jnp.bfloat16)
            summed = summed + rounded(jnp.dot(hidden, down, preferred_element_type=jnp.float32))
        total = total.at[flat_index].add(summed * weight_of[expert].reshape(-1)[:, None])
        return (total, None)
    start = jnp.zeros((count + 1, D), jnp.float32)
    total, ignored = lax.scan(per_expert, start, jnp.arange(EXPERTS, dtype=jnp.int32))
    return (wide + total[:count].reshape(NSEQ, LEN, D)).astype(jnp.bfloat16)
```

```python
import functools

import jax
import jax.numpy as jnp
from jax import lax
from jax.experimental import pallas as pl
from jax.experimental.pallas import tpu as pltpu
from jax.sharding import PartitionSpec as P

MESH = pl.DeviceIdType.MESH

D = 2048
QLEN = 128
QB = 128


EPSILON = 1e-05


def entering(value, axis, combine, identity):
    count, position = (lax.axis_size(axis), lax.axis_index(axis))
    everything = jax.tree.map(
        lambda part, kind: lax.all_gather(part.astype(kind), axis),
        value,
        (jnp.bfloat16, jnp.bfloat16),
    )
    start = jax.tree.map(
        lambda part, zero: jnp.broadcast_to(jnp.asarray(zero, part.dtype), part.shape),
        value,
        identity,
    )

    def hop(k, before):
        reached = k < position
        new = combine(
            before, jax.tree.map(lambda part, own: part[k].astype(own.dtype), everything, value)
        )
        return jax.tree.map(lambda a, b: jnp.where(reached, a, b), new, before)

    return lax.fori_loop(0, count, hop, start)


def join_states(earlier, later):
    return (earlier[0] * later[0], later[0][:, None, None] * earlier[1] + later[1])


def flip(index, offset, size):
    total, bit = 0, 1
    while bit < size:
        total = total + bit * ((index // bit + offset // bit) % 2)
        bit *= 2
    return total


def expert_kernel(
    sizes,
    picker_ref,
    expert_in_ref,
    gate_up_ref,
    gate_up_scale_ref,
    down_ref,
    down_scale_ref,
    high_ref,
    low_ref,
    stream_ref,
    out_ref,
    slots,
    w_gate_up,
    w_down,
    received,
    partial_out,
    partial_in,
    hidden,
    answers,
    returned,
    row_send,
    row_recv,
    part_send,
    part_recv,
    hid_send,
    hid_recv,
    ans_send,
    ans_recv,
):
    n_ctx, n_seq, n_tp = sizes
    sources = n_ctx * n_seq
    groups = sources // n_tp
    capacity, feature_width = slots.shape[1], slots.shape[2]
    half_width = w_down.shape[0]
    ctx, seq, tp = lax.axis_index("ctx"), lax.axis_index("seq"), lax.axis_index("tp")

    def at_offset(r):
        return flip(ctx, r % n_ctx, n_ctx), flip(seq, r // n_ctx, n_seq)

    def row_copy(r):
        c, s = at_offset(r)
        return pltpu.make_async_remote_copy(
            src_ref=slots.at[(c * n_seq + s) // 2],
            dst_ref=received.at[r],
            send_sem=row_send.at[r],
            recv_sem=row_recv.at[r],
            device_id={"ctx": c, "seq": s},
            device_id_type=MESH,
        )

    def part_copy(g, i):
        peer = lax.rem(tp + i, n_tp)
        return pltpu.make_async_remote_copy(
            src_ref=partial_out.at[g * n_tp + peer],
            dst_ref=partial_in.at[g * (n_tp - 1) + i - 1],
            send_sem=part_send.at[g * (n_tp - 1) + i - 1],
            recv_sem=part_recv.at[g * (n_tp - 1) + i - 1],
            device_id={"tp": peer},
            device_id_type=MESH,
        )

    def hid_copy(g, i):
        peer = lax.rem(tp + i, n_tp)
        return pltpu.make_async_remote_copy(
            src_ref=hidden.at[g * n_tp + tp],
            dst_ref=hidden.at[g * n_tp + tp],
            send_sem=hid_send.at[g * (n_tp - 1) + i - 1],
            recv_sem=hid_recv.at[g * (n_tp - 1) + i - 1],
            device_id={"tp": peer},
            device_id_type=MESH,
        )

    def hid_arrival(g, i):
        origin = lax.rem(tp + n_tp - i, n_tp)
        return pltpu.make_async_remote_copy(
            src_ref=hidden.at[g * n_tp + origin],
            dst_ref=hidden.at[g * n_tp + origin],
            send_sem=hid_send.at[g * (n_tp - 1) + i - 1],
            recv_sem=hid_recv.at[g * (n_tp - 1) + i - 1],
            device_id={"tp": origin},
            device_id_type=MESH,
        )

    def ans_copy(r):
        c, s = at_offset(r)
        return pltpu.make_async_remote_copy(
            src_ref=answers.at[r],
            dst_ref=returned.at[r],
            send_sem=ans_send.at[r],
            recv_sem=ans_recv.at[r],
            device_id={"ctx": c, "seq": s},
            device_id_type=MESH,
        )

    barrier = pltpu.get_barrier_semaphore()

    @pl.loop(1, sources)
    def _(r):
        c, s = at_offset(r)
        pl.semaphore_signal(barrier, inc=1, device_id={"ctx": c, "seq": s}, device_id_type=MESH)

    for i in range(1, n_tp):
        pl.semaphore_signal(
            barrier, inc=1, device_id={"tp": lax.rem(tp + i, n_tp)}, device_id_type=MESH
        )
    experts = slots.shape[0]
    slots[...] = (
        jnp.dot(picker_ref[...], expert_in_ref[...], preferred_element_type=jnp.float32)
        .astype(jnp.bfloat16)
        .reshape(experts, capacity, feature_width)
    )
    pl.semaphore_wait(barrier, sources + n_tp - 2)

    @pl.loop(1, sources)
    def _(r):
        row_copy(r).start()

    received[0] = slots[(ctx * n_seq + seq) // 2]

    @pl.loop(0, feature_width // QB)
    def _(i):
        rows = pl.ds(pl.multiple_of(i * QB, QB), QB)
        for kind in range(2):
            for j in range(half_width // QB):
                w_gate_up[rows, kind * half_width + j * QB : kind * half_width + (j + 1) * QB] = (
                    gate_up_ref[kind, rows, j * QB : (j + 1) * QB].astype(jnp.float32)
                    * gate_up_scale_ref[kind, i, j]
                ).astype(jnp.bfloat16)

    @pl.loop(0, half_width // QB)
    def _(i):
        rows = pl.ds(pl.multiple_of(i * QB, QB), QB)
        for j in range(feature_width // QB):
            w_down[rows, j * QB : (j + 1) * QB] = (
                down_ref[rows, j * QB : (j + 1) * QB].astype(jnp.float32) * down_scale_ref[i, j]
            ).astype(jnp.bfloat16)

    @pl.loop(0, groups + 2)
    def _(step):
        @pl.when(step < groups)
        def _():
            g = step
            for i in range(n_tp):
                r = g * n_tp + i
                if i == 0:

                    @pl.when(g > 0)
                    def _():
                        row_copy(r).wait_recv()
                else:
                    row_copy(r).wait_recv()
            rows = received[pl.ds(g * n_tp, n_tp)].reshape(n_tp * capacity, feature_width)
            both = jnp.dot(rows, w_gate_up[...], preferred_element_type=jnp.float32)
            partial_out[pl.ds(g * n_tp, n_tp)] = both.astype(jnp.bfloat16).reshape(
                n_tp, capacity, 2 * half_width
            )
            for i in range(1, n_tp):
                part_copy(g, i).start()

        @pl.when((step >= 1) & (step < groups + 1))
        def _():
            g = step - 1
            total = partial_out[g * n_tp + tp].astype(jnp.float32)
            for i in range(1, n_tp):
                part_copy(g, i).wait_recv()
                total = total + partial_in[g * (n_tp - 1) + i - 1].astype(jnp.float32)
            gate, up = total[:, :half_width], total[:, half_width:]
            hidden[g * n_tp + tp] = (gate / (1.0 + jnp.exp(-gate)) * up).astype(jnp.bfloat16)
            for i in range(1, n_tp):
                hid_copy(g, i).start()

        @pl.when(step >= 2)
        def _():
            g = step - 2
            for i in range(1, n_tp):
                hid_arrival(g, i).wait_recv()
            rows = hidden[pl.ds(g * n_tp, n_tp)].reshape(n_tp * capacity, half_width)
            answer = jnp.dot(rows, w_down[...], preferred_element_type=jnp.float32)
            answers[pl.ds(g * n_tp, n_tp)] = answer.astype(jnp.bfloat16).reshape(
                n_tp, capacity, feature_width
            )
            for i in range(n_tp):
                r = g * n_tp + i
                if i == 0:

                    @pl.when(g > 0)
                    def _():
                        ans_copy(r).start()
                else:
                    ans_copy(r).start()

    returned[0] = answers[0]

    @pl.loop(1, sources)
    def _(r):
        ans_copy(r).wait_recv()

    back = returned[...].reshape(sources * capacity, feature_width)
    mixed = jnp.dot(high_ref[...], back, preferred_element_type=jnp.float32)
    mixed = mixed + jnp.dot(low_ref[...], back, preferred_element_type=jnp.float32)
    out_ref[...] = (stream_ref[...].astype(jnp.float32) + mixed).astype(jnp.bfloat16)

    @pl.loop(1, sources)
    def _(r):
        row_copy(r).wait_send()
        ans_copy(r).wait_send()

    @pl.loop(0, groups)
    def _(g):
        for i in range(1, n_tp):
            part_copy(g, i).wait_send()
            hid_copy(g, i).wait_send()


def expert_layer(picker, expert_in, gate_up, gate_up_scale, down, down_scale, high, low, stream):
    sizes = tuple(lax.axis_size(axis) for axis in ("ctx", "seq", "tp"))
    sources, n_tp = sizes[0] * sizes[1], sizes[2]
    groups = sources // n_tp
    experts = sources // 2
    tokens, feature_width = expert_in.shape
    capacity = picker.shape[0] // experts
    half_width = down.shape[0]
    vmem, smem = pl.BlockSpec(memory_space=pltpu.VMEM), pl.BlockSpec(memory_space=pltpu.SMEM)
    shares = groups * (n_tp - 1)
    dma = pltpu.SemaphoreType.DMA
    return pl.pallas_call(
        functools.partial(expert_kernel, sizes),
        out_shape=jax.ShapeDtypeStruct((tokens, feature_width), jnp.bfloat16),
        in_specs=[vmem, vmem, vmem, smem, vmem, smem, vmem, vmem, vmem],
        out_specs=vmem,
        scratch_shapes=[
            pltpu.VMEM((experts, capacity, feature_width), jnp.bfloat16),
            pltpu.VMEM((feature_width, 2 * half_width), jnp.bfloat16),
            pltpu.VMEM((half_width, feature_width), jnp.bfloat16),
            pltpu.VMEM((sources, capacity, feature_width), jnp.bfloat16),
            pltpu.VMEM((sources, capacity, 2 * half_width), jnp.bfloat16),
            pltpu.VMEM((shares, capacity, 2 * half_width), jnp.bfloat16),
            pltpu.VMEM((sources, capacity, half_width), jnp.bfloat16),
            pltpu.VMEM((sources, capacity, feature_width), jnp.bfloat16),
            pltpu.VMEM((sources, capacity, feature_width), jnp.bfloat16),
            dma((sources,)),
            dma((sources,)),
            dma((shares,)),
            dma((shares,)),
            dma((shares,)),
            dma((shares,)),
            dma((sources,)),
            dma((sources,)),
        ],
        compiler_params=pltpu.CompilerParams(
            collective_id=1, has_side_effects=True, vmem_limit_bytes=56 * 1024 * 1024
        ),
    )(picker, expert_in, gate_up, gate_up_scale, down, down_scale, high, low, stream)


def on_device(
    inputs,
    gating,
    write_proj,
    read_proj,
    step_raw,
    decay_log,
    skip_gain,
    norm_gain,
    out_weight,
    residual,
    routes,
    route_weight,
    layer_gain,
    gate_up_codes,
    gate_up_scales,
    down_codes,
    down_scales,
):
    tokens_here = inputs.shape[1]
    heads_here = step_raw.shape[2]
    groups_here = write_proj.shape[2]
    state_width = write_proj.shape[3]
    head_width = inputs.shape[2] // heads_here
    per_group = heads_here // groups_here
    blocks = tokens_here // QLEN
    values = inputs[0].reshape(blocks, QLEN, heads_here, head_width)
    writes = write_proj[0].reshape(blocks, QLEN, groups_here, state_width)
    reads = read_proj[0].reshape(blocks, QLEN, groups_here, state_width)
    stride_size = jax.nn.softplus(step_raw[0]).reshape(blocks, QLEN, heads_here)
    rate = -jnp.exp(decay_log)
    causal_mask = jnp.arange(QLEN)[:, None] >= jnp.arange(QLEN)[None, :]
    lower = causal_mask.astype(jnp.float32)
    cumul = jnp.einsum(
        "ts,bsh->bth", lower, stride_size * rate[None, None, :], precision=lax.Precision.HIGHEST
    )
    scores = jnp.einsum("btgn,bsgn->bgts", reads, writes, preferred_element_type=jnp.float32)
    scores = jnp.repeat(scores, per_group, axis=1)
    cum_heads = jnp.swapaxes(cumul, 1, 2)
    spread = cum_heads[:, :, :, None] - cum_heads[:, :, None, :]
    decay = (
        jnp.where(causal_mask, jnp.exp(jnp.where(causal_mask, spread, 0.0)), 0.0)
        * jnp.swapaxes(stride_size, 1, 2)[:, :, None, :]
    )
    mixing = (scores * decay).astype(jnp.bfloat16)
    local = jnp.einsum("bhts,bshp->bthp", mixing, values, preferred_element_type=jnp.float32)
    final = cumul[:, -1, :]
    coefficient_array = jnp.exp(final[:, None, :] - cumul) * stride_size
    weighted = (values.astype(jnp.float32) * coefficient_array[..., None]).astype(jnp.bfloat16)
    write_heads = jnp.repeat(writes, per_group, axis=2)
    contrib = jnp.einsum(
        "bshp,bshn->bhpn", weighted, write_heads, preferred_element_type=jnp.float32
    )
    keep = jnp.exp(final)
    total_keep = jnp.ones((heads_here,), jnp.float32)
    state_total = jnp.zeros((heads_here, head_width, state_width), jnp.float32)
    state_total = keep[0][:, None, None] * state_total + contrib[0]
    total_keep = total_keep * keep[0]
    identity = (
        jnp.ones((heads_here,), jnp.float32),
        jnp.zeros((heads_here, head_width, state_width), jnp.float32),
    )
    incoming_flow = entering((total_keep, state_total), "ctx", join_states, identity)[1]
    starts = []
    starts.append(incoming_flow)
    starts = jnp.stack(starts)
    read_heads = jnp.repeat(reads, per_group, axis=2).astype(jnp.float32)
    carried = jnp.einsum("bhpn,bthn->bthp", starts, read_heads, precision=lax.Precision.HIGHEST)
    output = (
        local
        + jnp.exp(cumul)[..., None] * carried
        + skip_gain[None, None, :, None] * values.astype(jnp.float32)
    )
    gated = output.reshape(tokens_here, -1) * jax.nn.silu(gating[0].astype(jnp.float32))
    grouped = gated.reshape(tokens_here, groups_here, -1)
    normed = (
        grouped * lax.rsqrt(jnp.mean(grouped * grouped, axis=-1, keepdims=True) + EPSILON)
    ).reshape(tokens_here, -1)
    normed = (normed * norm_gain).astype(jnp.bfloat16)
    partial_value = jnp.dot(
        normed,
        lax.all_gather(out_weight, "ctx", axis=1, tiled=True),
        preferred_element_type=jnp.float32,
    )
    mixer = lax.psum_scatter(
        partial_value.astype(jnp.bfloat16), "tp", scatter_dimension=1, tiled=True
    ).astype(jnp.float32)
    stream = (residual[0].astype(jnp.float32) + mixer).astype(jnp.bfloat16)
    wide = stream.astype(jnp.float32)
    squares = lax.psum(jnp.sum(wide * wide, axis=-1), "tp")
    expert_in = (wide * lax.rsqrt(squares / D + EPSILON)[:, None] * layer_gain).astype(jnp.bfloat16)
    n_ctx, n_seq = lax.axis_size("ctx"), lax.axis_size("seq")
    experts = n_ctx * n_seq // 2
    capacity = -(-(3 * tokens_here // experts) // 16) * 16
    chosen = routes[0].reshape(-1)
    pair_count = chosen.shape[0]
    ordinal = jnp.arange(pair_count)
    rank = jnp.sum(
        (chosen[:, None] == chosen[None, :]) & (ordinal[None, :] < ordinal[:, None]), axis=1
    )
    target = (chosen * capacity + rank).reshape(tokens_here, 2)
    column = jnp.arange(experts * capacity)
    picker = jnp.any(column[:, None, None] == target[None], axis=-1).astype(jnp.bfloat16)
    offset = jnp.arange(2 * experts)
    holder = flip(lax.axis_index("ctx"), offset % n_ctx, n_ctx) * n_seq + flip(
        lax.axis_index("seq"), offset // n_ctx, n_seq
    )
    place = ((holder // 2)[:, None] * capacity + jnp.arange(capacity)[None, :]).reshape(-1)
    weights = jnp.sum(
        jnp.where(place[None, :, None] == target[:, None, :], route_weight[0][:, None, :], 0.0),
        axis=-1,
    )
    high = weights.astype(jnp.bfloat16)
    low = (weights - high.astype(jnp.float32)).astype(jnp.bfloat16)
    return expert_layer(
        picker,
        expert_in,
        gate_up_codes[0],
        gate_up_scales[0],
        down_codes[0],
        down_scales[0],
        high,
        low,
        stream,
    )[None]


def solution(mesh):
    placed = (
        P("seq", "ctx", "tp"),
        P("seq", "ctx", "tp"),
        P("seq", "ctx", "tp", None),
        P("seq", "ctx", "tp", None),
        P("seq", "ctx", "tp"),
        P("tp"),
        P("tp"),
        P("tp"),
        P("tp", "ctx"),
        P("seq", "ctx", "tp"),
        P("seq", "ctx", None),
        P("seq", "ctx", None),
        P("tp"),
        P(("ctx", "seq"), None, "tp", None),
        P(("ctx", "seq"), None, "tp", None),
        P(("ctx", "seq"), None, "tp"),
        P(("ctx", "seq"), None, "tp"),
    )
    return jax.shard_map(
        on_device, mesh=mesh, in_specs=placed, out_specs=P("seq", "ctx", "tp"), check_vma=False
    )
```

```python
import functools

import jax
import jax.numpy as jnp
from jax import lax
from jax.experimental import pallas as pl
from jax.experimental.pallas import tpu as pltpu
from jax.sharding import PartitionSpec as P

MESH = pl.DeviceIdType.MESH

QB = 128


EPSILON = 1e-05


def flip(index, offset, size):
    total, bit = 0, 1
    while bit < size:
        total = total + bit * ((index // bit + offset // bit) % 2)
        bit *= 2
    return total


def expert_kernel(
    sizes,
    picker_ref,
    expert_in_ref,
    gate_up_ref,
    gate_up_scale_ref,
    down_ref,
    down_scale_ref,
    high_ref,
    low_ref,
    stream_ref,
    out_ref,
    slots,
    w_gate_up,
    w_down,
    received,
    partial_out,
    partial_in,
    hidden,
    answers,
    returned,
    row_send,
    row_recv,
    part_send,
    part_recv,
    hid_send,
    hid_recv,
    ans_send,
    ans_recv,
):
    n_ctx, n_seq, n_tp = sizes
    sources = n_ctx * n_seq
    groups = sources // n_tp
    capacity, feature_width = slots.shape[1], slots.shape[2]
    half_width = w_down.shape[0]
    ctx, seq, tp = lax.axis_index("ctx"), lax.axis_index("seq"), lax.axis_index("tp")

    def at_offset(r):
        return flip(ctx, r % n_ctx, n_ctx), flip(seq, r // n_ctx, n_seq)

    def row_copy(r):
        c, s = at_offset(r)
        return pltpu.make_async_remote_copy(
            src_ref=slots.at[(c * n_seq + s) // 2],
            dst_ref=received.at[r],
            send_sem=row_send.at[r],
            recv_sem=row_recv.at[r],
            device_id={"ctx": c, "seq": s},
            device_id_type=MESH,
        )

    def part_copy(g, i):
        peer = lax.rem(tp + i, n_tp)
        return pltpu.make_async_remote_copy(
            src_ref=partial_out.at[g * n_tp + peer],
            dst_ref=partial_in.at[g * (n_tp - 1) + i - 1],
            send_sem=part_send.at[g * (n_tp - 1) + i - 1],
            recv_sem=part_recv.at[g * (n_tp - 1) + i - 1],
            device_id={"tp": peer},
            device_id_type=MESH,
        )

    def hid_copy(g, i):
        peer = lax.rem(tp + i, n_tp)
        return pltpu.make_async_remote_copy(
            src_ref=hidden.at[g * n_tp + tp],
            dst_ref=hidden.at[g * n_tp + tp],
            send_sem=hid_send.at[g * (n_tp - 1) + i - 1],
            recv_sem=hid_recv.at[g * (n_tp - 1) + i - 1],
            device_id={"tp": peer},
            device_id_type=MESH,
        )

    def hid_arrival(g, i):
        origin = lax.rem(tp + n_tp - i, n_tp)
        return pltpu.make_async_remote_copy(
            src_ref=hidden.at[g * n_tp + origin],
            dst_ref=hidden.at[g * n_tp + origin],
            send_sem=hid_send.at[g * (n_tp - 1) + i - 1],
            recv_sem=hid_recv.at[g * (n_tp - 1) + i - 1],
            device_id={"tp": origin},
            device_id_type=MESH,
        )

    def ans_copy(r):
        c, s = at_offset(r)
        return pltpu.make_async_remote_copy(
            src_ref=answers.at[r],
            dst_ref=returned.at[r],
            send_sem=ans_send.at[r],
            recv_sem=ans_recv.at[r],
            device_id={"ctx": c, "seq": s},
            device_id_type=MESH,
        )

    barrier = pltpu.get_barrier_semaphore()

    @pl.loop(1, sources)
    def _(r):
        c, s = at_offset(r)
        pl.semaphore_signal(barrier, inc=1, device_id={"ctx": c, "seq": s}, device_id_type=MESH)

    for i in range(1, n_tp):
        pl.semaphore_signal(
            barrier, inc=1, device_id={"tp": lax.rem(tp + i, n_tp)}, device_id_type=MESH
        )
    experts = slots.shape[0]
    slots[...] = (
        jnp.dot(picker_ref[...], expert_in_ref[...], preferred_element_type=jnp.float32)
        .astype(jnp.bfloat16)
        .reshape(experts, capacity, feature_width)
    )
    pl.semaphore_wait(barrier, sources + n_tp - 2)

    @pl.loop(1, sources)
    def _(r):
        row_copy(r).start()

    received[0] = slots[(ctx * n_seq + seq) // 2]

    @pl.loop(0, feature_width // QB)
    def _(i):
        rows = pl.ds(pl.multiple_of(i * QB, QB), QB)
        for kind in range(2):
            for j in range(half_width // QB):
                w_gate_up[rows, kind * half_width + j * QB : kind * half_width + (j + 1) * QB] = (
                    gate_up_ref[kind, rows, j * QB : (j + 1) * QB].astype(jnp.float32)
                    * gate_up_scale_ref[kind, i, j]
                ).astype(jnp.bfloat16)

    @pl.loop(0, half_width // QB)
    def _(i):
        rows = pl.ds(pl.multiple_of(i * QB, QB), QB)
        for j in range(feature_width // QB):
            w_down[rows, j * QB : (j + 1) * QB] = (
                down_ref[rows, j * QB : (j + 1) * QB].astype(jnp.float32) * down_scale_ref[i, j]
            ).astype(jnp.bfloat16)

    @pl.loop(0, groups + 2)
    def _(step):
        @pl.when(step < groups)
        def _():
            g = step
            for i in range(n_tp):
                r = g * n_tp + i
                if i == 0:

                    @pl.when(g > 0)
                    def _():
                        row_copy(r).wait_recv()
                else:
                    row_copy(r).wait_recv()
            rows = received[pl.ds(g * n_tp, n_tp)].reshape(n_tp * capacity, feature_width)
            both = jnp.dot(rows, w_gate_up[...], preferred_element_type=jnp.float32)
            partial_out[pl.ds(g * n_tp, n_tp)] = both.astype(jnp.bfloat16).reshape(
                n_tp, capacity, 2 * half_width
            )
            for i in range(1, n_tp):
                part_copy(g, i).start()

        @pl.when((step >= 1) & (step < groups + 1))
        def _():
            g = step - 1
            total = partial_out[g * n_tp + tp].astype(jnp.float32)
            for i in range(1, n_tp):
                part_copy(g, i).wait_recv()
                total = total + partial_in[g * (n_tp - 1) + i - 1].astype(jnp.float32)
            gate, up = total[:, :half_width], total[:, half_width:]
            hidden[g * n_tp + tp] = (gate / (1.0 + jnp.exp(-gate)) * up).astype(jnp.bfloat16)
            for i in range(1, n_tp):
                hid_copy(g, i).start()

        @pl.when(step >= 2)
        def _():
            g = step - 2
            for i in range(1, n_tp):
                hid_arrival(g, i).wait_recv()
            rows = hidden[pl.ds(g * n_tp, n_tp)].reshape(n_tp * capacity, half_width)
            answer = jnp.dot(rows, w_down[...], preferred_element_type=jnp.float32)
            answers[pl.ds(g * n_tp, n_tp)] = answer.astype(jnp.bfloat16).reshape(
                n_tp, capacity, feature_width
            )
            for i in range(n_tp):
                r = g * n_tp + i
                if i == 0:

                    @pl.when(g > 0)
                    def _():
                        ans_copy(r).start()
                else:
                    ans_copy(r).start()

    returned[0] = answers[0]

    @pl.loop(1, sources)
    def _(r):
        ans_copy(r).wait_recv()

    back = returned[...].reshape(sources * capacity, feature_width)
    mixed = jnp.dot(high_ref[...], back, preferred_element_type=jnp.float32)
    mixed = mixed + jnp.dot(low_ref[...], back, preferred_element_type=jnp.float32)
    out_ref[...] = (stream_ref[...].astype(jnp.float32) + mixed).astype(jnp.bfloat16)

    @pl.loop(1, sources)
    def _(r):
        row_copy(r).wait_send()
        ans_copy(r).wait_send()

    @pl.loop(0, groups)
    def _(g):
        for i in range(1, n_tp):
            part_copy(g, i).wait_send()
            hid_copy(g, i).wait_send()


def expert_layer(picker, expert_in, gate_up, gate_up_scale, down, down_scale, high, low, stream):
    sizes = tuple(lax.axis_size(axis) for axis in ("ctx", "seq", "tp"))
    sources, n_tp = sizes[0] * sizes[1], sizes[2]
    groups = sources // n_tp
    experts = sources // 2
    tokens, feature_width = expert_in.shape
    capacity = picker.shape[0] // experts
    half_width = down.shape[0]
    vmem, smem = pl.BlockSpec(memory_space=pltpu.VMEM), pl.BlockSpec(memory_space=pltpu.SMEM)
    shares = groups * (n_tp - 1)
    dma = pltpu.SemaphoreType.DMA
    return pl.pallas_call(
        functools.partial(expert_kernel, sizes),
        out_shape=jax.ShapeDtypeStruct((tokens, feature_width), jnp.bfloat16),
        in_specs=[vmem, vmem, vmem, smem, vmem, smem, vmem, vmem, vmem],
        out_specs=vmem,
        scratch_shapes=[
            pltpu.VMEM((experts, capacity, feature_width), jnp.bfloat16),
            pltpu.VMEM((feature_width, 2 * half_width), jnp.bfloat16),
            pltpu.VMEM((half_width, feature_width), jnp.bfloat16),
            pltpu.VMEM((sources, capacity, feature_width), jnp.bfloat16),
            pltpu.VMEM((sources, capacity, 2 * half_width), jnp.bfloat16),
            pltpu.VMEM((shares, capacity, 2 * half_width), jnp.bfloat16),
            pltpu.VMEM((sources, capacity, half_width), jnp.bfloat16),
            pltpu.VMEM((sources, capacity, feature_width), jnp.bfloat16),
            pltpu.VMEM((sources, capacity, feature_width), jnp.bfloat16),
            dma((sources,)),
            dma((sources,)),
            dma((shares,)),
            dma((shares,)),
            dma((shares,)),
            dma((shares,)),
            dma((sources,)),
            dma((sources,)),
        ],
        compiler_params=pltpu.CompilerParams(
            collective_id=1, has_side_effects=True, vmem_limit_bytes=56 * 1024 * 1024
        ),
    )(picker, expert_in, gate_up, gate_up_scale, down, down_scale, high, low, stream)


def mixer_kernel(
    sizes,
    value_ref,
    gating_ref,
    write_ref,
    read_ref,
    step_ref,
    decay_ref,
    skip_ref,
    norm_gain_ref,
    out_weight_ref,
    residual_ref,
    layer_gain_ref,
    stream_ref,
    expert_in_ref,
    contrib,
    state_in,
    state_out,
    rows_in,
    product,
    mixed_out,
    mixed_in,
    square_out,
    square_in,
    state_send,
    state_recv,
    rows_send,
    rows_recv,
    mixed_send,
    mixed_recv,
    square_send,
    square_recv,
):
    n_ctx, _, n_tp = sizes
    ctx, tp = lax.axis_index("ctx"), lax.axis_index("tp")
    tokens, channels = value_ref.shape
    heads = step_ref.shape[1]
    groups, span = rows_in.shape[0], rows_in.shape[3]
    head_width = channels // heads
    per_group = heads // groups
    state_width = write_ref.shape[1] // groups
    columns, features = out_weight_ref.shape[1], residual_ref.shape[1]
    owners = features // columns
    pair = 2 * head_width
    f32, bf16 = jnp.float32, jnp.bfloat16

    def state_copy(g, target):
        return pltpu.make_async_remote_copy(
            src_ref=state_out.at[g],
            dst_ref=state_in.at[g],
            send_sem=state_send.at[g],
            recv_sem=state_recv.at[g],
            device_id={"ctx": target},
            device_id_type=MESH,
        )

    def rows_copy(g, source, slot, offset):
        return pltpu.make_async_remote_copy(
            src_ref=rows_in.at[g, source],
            dst_ref=rows_in.at[g, slot],
            send_sem=rows_send.at[g * n_ctx + slot],
            recv_sem=rows_recv.at[g * n_ctx + slot],
            device_id={"ctx": flip(ctx, offset, n_ctx)},
            device_id_type=MESH,
        )

    target_tp = ctx // owners

    def mixed_copy(a, slot):
        return pltpu.make_async_remote_copy(
            src_ref=mixed_out.at[a],
            dst_ref=mixed_in.at[slot],
            send_sem=mixed_send.at[a],
            recv_sem=mixed_recv.at[slot],
            device_id={"ctx": flip(ctx, a, n_ctx), "tp": target_tp},
            device_id_type=MESH,
        )

    def square_copy(i):
        return pltpu.make_async_remote_copy(
            src_ref=square_out,
            dst_ref=square_in.at[i - 1],
            send_sem=square_send.at[i - 1],
            recv_sem=square_recv.at[i - 1],
            device_id={"tp": lax.rem(tp + i, n_tp)},
            device_id_type=MESH,
        )

    barrier = pltpu.get_barrier_semaphore()
    for a in range(n_ctx):
        for i in range(n_tp):
            if a + i > 0:
                pl.semaphore_signal(
                    barrier,
                    inc=1,
                    device_id={"ctx": flip(ctx, a, n_ctx), "tp": lax.rem(tp + i, n_tp)},
                    device_id_type=MESH,
                )

    step = step_ref[...]
    stride = jnp.maximum(step, 0.0) + jnp.log1p(jnp.exp(-jnp.abs(step)))
    at_row = lax.broadcasted_iota(jnp.int32, (tokens, tokens), 0)
    at_col = lax.broadcasted_iota(jnp.int32, (tokens, tokens), 1)
    causal = at_row >= at_col
    cumul = jnp.dot(
        causal.astype(f32), stride * -jnp.exp(decay_ref[...]), precision=lax.Precision.HIGHEST
    )
    cumul_t, stride_t = cumul.T, stride.T
    final = cumul[tokens - 1 : tokens, :]
    coefficient = jnp.exp(final - cumul) * stride
    keep = jnp.exp(final)
    growth = jnp.exp(cumul)
    first_half = lax.broadcasted_iota(jnp.int32, (tokens, pair), 1) < head_width

    def widen(table, g):
        return jnp.concatenate(
            [
                jnp.where(first_half, table[:, h : h + 1], table[:, h + 1 : h + 2])
                for h in range(g * per_group, (g + 1) * per_group, 2)
            ],
            axis=1,
        )

    for g in range(groups):
        lanes = slice(g * span, (g + 1) * span)
        weighted = (value_ref[:, lanes].astype(f32) * widen(coefficient, g)).astype(bf16)
        contrib[g] = lax.dot_general(
            weighted,
            write_ref[:, g * state_width : (g + 1) * state_width],
            (((0,), (0,)), ((), ())),
            preferred_element_type=f32,
        )

    pl.semaphore_wait(barrier, n_ctx * n_tp - 1)

    @pl.when(ctx == 0)
    def _():
        state_in[...] = jnp.zeros_like(state_in)

    for g in range(groups):
        lanes = slice(g * span, (g + 1) * span)
        narrow = slice(g * state_width, (g + 1) * state_width)
        values = value_ref[:, lanes]
        scores = lax.dot_general(
            read_ref[:, narrow],
            write_ref[:, narrow],
            (((1,), (1,)), ((), ())),
            preferred_element_type=f32,
        )
        local = []
        for k in range(per_group // 2):
            block = values[:, k * pair : (k + 1) * pair]
            mixing = []
            for h in (g * per_group + 2 * k, g * per_group + 2 * k + 1):
                spread = cumul[:, h : h + 1] - cumul_t[h : h + 1, :]
                decay = jnp.exp(jnp.where(causal, spread, -jnp.inf)) * stride_t[h : h + 1, :]
                mixing.append((scores * decay).astype(bf16))
            zero = jnp.zeros_like(block)
            local.append(
                jnp.dot(
                    jnp.concatenate(mixing, axis=1),
                    jnp.concatenate(
                        [jnp.where(first_half, block, zero), jnp.where(first_half, zero, block)],
                        axis=0,
                    ),
                    preferred_element_type=f32,
                )
            )

        @pl.when(ctx > 0)
        def _():
            state_copy(g, ctx - 1).wait_recv()

        @pl.when(ctx < n_ctx - 1)
        def _():
            for j in range(per_group):
                h = g * per_group + j
                part = slice(j * head_width, (j + 1) * head_width)
                state_out[g, part, :] = (
                    state_in[g, part, :].astype(f32) * keep[:, h : h + 1] + contrib[g, part, :]
                ).astype(bf16)
            state_copy(g, ctx + 1).start()

        carried = lax.dot_general(
            read_ref[:, narrow],
            state_in[g],
            (((1,), (1,)), ((), ())),
            preferred_element_type=f32,
        )
        skip = jnp.concatenate(
            [
                jnp.where(first_half, skip_ref[h], skip_ref[h + 1])
                for h in range(g * per_group, (g + 1) * per_group, 2)
            ],
            axis=1,
        )
        output = (
            jnp.concatenate(local, axis=1)
            + widen(growth, g) * carried
            + skip * values.astype(f32)
        )
        gate = gating_ref[:, lanes].astype(f32)
        gated = output * (gate / (1.0 + jnp.exp(-gate)))
        scale = lax.rsqrt(jnp.mean(gated * gated, axis=1, keepdims=True) + EPSILON)
        rows_in[g, 0] = (gated * scale * norm_gain_ref[:, lanes]).astype(bf16)
        for a in range(2, n_ctx, 2):
            rows_copy(g, 0, a, a).start()
        rows_copy(g, 0, 1, 1).start()

    def multiply(g):
        for a in range(1, n_ctx, 2):
            rows_copy(g, 0, a, a).wait_recv()
        part = jnp.dot(
            rows_in[g].reshape(n_ctx * tokens, span),
            out_weight_ref[g * span : (g + 1) * span, :],
            preferred_element_type=f32,
        )
        if g > 0:
            part = part + product[...]
        if g < groups - 1:
            product[...] = part
        else:
            mixed_out[...] = part.astype(bf16).reshape(n_ctx, tokens, columns)

    for g in range(groups):
        for a in range(2, n_ctx, 2):
            rows_copy(g, 0, a, a).wait_recv()
            rows_copy(g, a, a + 1, 1).start()
        if g > 0:
            multiply(g - 1)
    multiply(groups - 1)

    own_slot = lax.rem(ctx, owners) * n_tp + tp
    for a in range(1, n_ctx):
        mixed_copy(a, own_slot).start()

    @pl.when(tp == target_tp)
    def _():
        mixed_in[own_slot] = mixed_out[0]

    @pl.when(tp != target_tp)
    def _():
        mixed_copy(0, own_slot).start()

    squares = jnp.zeros((tokens, 1), f32)
    for q in range(owners):
        lanes = slice(q * columns, (q + 1) * columns)
        total = residual_ref[:, lanes].astype(f32)
        for i in range(n_tp):

            @pl.when((ctx != tp * owners + q) | (tp != i))
            def _():
                mixed_copy(1, q * n_tp + i).wait_recv()

            total = total + mixed_in[q * n_tp + i].astype(f32)
        total = total.astype(bf16)
        stream_ref[:, lanes] = total
        total = total.astype(f32)
        squares = squares + jnp.sum(total * total, axis=1, keepdims=True)
    across = jnp.broadcast_to(squares, (tokens, tokens)).T[:8]
    square_out[...] = across
    for i in range(1, n_tp):
        square_copy(i).start()
    for i in range(1, n_tp):
        square_copy(i).wait_recv()
        across = across + square_in[i - 1]
    squares = jnp.broadcast_to(across[:1], (tokens, tokens)).T[:, :1]
    scale = lax.rsqrt(squares / (features * n_tp) + EPSILON)
    expert_in_ref[...] = (stream_ref[...].astype(f32) * scale * layer_gain_ref[...]).astype(bf16)

    for i in range(1, n_tp):
        square_copy(i).wait_send()
    for a in range(1, n_ctx):
        mixed_copy(a, own_slot).wait_send()

    @pl.when(tp != target_tp)
    def _():
        mixed_copy(0, own_slot).wait_send()

    for g in range(groups):
        for a in range(1, n_ctx):
            rows_copy(g, 0, a, a).wait_send()

    @pl.when(ctx < n_ctx - 1)
    def _():
        for g in range(groups):
            state_copy(g, ctx + 1).wait_send()


def mixer_layer(
    values, gating, writes, reads, step, decay, skip, norm_gain, out_weight, residual, layer_gain
):
    sizes = tuple(lax.axis_size(axis) for axis in ("ctx", "seq", "tp"))
    n_ctx, _, n_tp = sizes
    tokens, channels = values.shape
    groups, state_width = writes.shape[1], writes.shape[2]
    span = channels // groups
    columns, features = out_weight.shape[1], residual.shape[1]
    vmem, smem = pl.BlockSpec(memory_space=pltpu.VMEM), pl.BlockSpec(memory_space=pltpu.SMEM)
    slots = features // columns * n_tp
    dma = pltpu.SemaphoreType.DMA
    out = jax.ShapeDtypeStruct((tokens, features), jnp.bfloat16)
    return pl.pallas_call(
        functools.partial(mixer_kernel, sizes),
        out_shape=(out, out),
        in_specs=[vmem] * 6 + [smem] + [vmem] * 4,
        out_specs=(vmem, vmem),
        scratch_shapes=[
            pltpu.VMEM((groups, span, state_width), jnp.float32),
            pltpu.VMEM((groups, span, state_width), jnp.bfloat16),
            pltpu.VMEM((groups, span, state_width), jnp.bfloat16),
            pltpu.VMEM((groups, n_ctx, tokens, span), jnp.bfloat16),
            pltpu.VMEM((n_ctx * tokens, columns), jnp.float32),
            pltpu.VMEM((n_ctx, tokens, columns), jnp.bfloat16),
            pltpu.VMEM((slots, tokens, columns), jnp.bfloat16),
            pltpu.VMEM((8, tokens), jnp.float32),
            pltpu.VMEM((n_tp - 1, 8, tokens), jnp.float32),
            dma((groups,)),
            dma((groups,)),
            dma((groups * n_ctx,)),
            dma((groups * n_ctx,)),
            dma((n_ctx,)),
            dma((slots,)),
            dma((n_tp - 1,)),
            dma((n_tp - 1,)),
        ],
        compiler_params=pltpu.CompilerParams(
            collective_id=2, has_side_effects=True, vmem_limit_bytes=48 * 1024 * 1024
        ),
    )(
        values,
        gating,
        writes.reshape(tokens, groups * state_width),
        reads.reshape(tokens, groups * state_width),
        step,
        decay[None],
        skip,
        norm_gain[None],
        out_weight,
        residual,
        layer_gain[None],
    )


def on_device(
    inputs,
    gating,
    write_proj,
    read_proj,
    step_raw,
    decay_log,
    skip_gain,
    norm_gain,
    out_weight,
    residual,
    routes,
    route_weight,
    layer_gain,
    gate_up_codes,
    gate_up_scales,
    down_codes,
    down_scales,
):
    tokens_here = inputs.shape[1]
    stream, expert_in = mixer_layer(
        inputs[0],
        gating[0],
        write_proj[0],
        read_proj[0],
        step_raw[0],
        decay_log,
        skip_gain,
        norm_gain,
        out_weight,
        residual[0],
        layer_gain,
    )
    n_ctx, n_seq = lax.axis_size("ctx"), lax.axis_size("seq")
    experts = n_ctx * n_seq // 2
    capacity = -(-(3 * tokens_here // experts) // 16) * 16
    chosen = routes[0].reshape(-1)
    pair_count = chosen.shape[0]
    ordinal = jnp.arange(pair_count)
    rank = jnp.sum(
        (chosen[:, None] == chosen[None, :]) & (ordinal[None, :] < ordinal[:, None]), axis=1
    )
    target = (chosen * capacity + rank).reshape(tokens_here, 2)
    column = jnp.arange(experts * capacity)
    picker = jnp.any(column[:, None, None] == target[None], axis=-1).astype(jnp.bfloat16)
    offset = jnp.arange(2 * experts)
    holder = flip(lax.axis_index("ctx"), offset % n_ctx, n_ctx) * n_seq + flip(
        lax.axis_index("seq"), offset // n_ctx, n_seq
    )
    place = ((holder // 2)[:, None] * capacity + jnp.arange(capacity)[None, :]).reshape(-1)
    weights = jnp.sum(
        jnp.where(place[None, :, None] == target[:, None, :], route_weight[0][:, None, :], 0.0),
        axis=-1,
    )
    high = weights.astype(jnp.bfloat16)
    low = (weights - high.astype(jnp.float32)).astype(jnp.bfloat16)
    return expert_layer(
        picker,
        expert_in,
        gate_up_codes[0],
        gate_up_scales[0],
        down_codes[0],
        down_scales[0],
        high,
        low,
        stream,
    )[None]


def solution(mesh):
    placed = (
        P("seq", "ctx", "tp"),
        P("seq", "ctx", "tp"),
        P("seq", "ctx", "tp", None),
        P("seq", "ctx", "tp", None),
        P("seq", "ctx", "tp"),
        P("tp"),
        P("tp"),
        P("tp"),
        P("tp", "ctx"),
        P("seq", "ctx", "tp"),
        P("seq", "ctx", None),
        P("seq", "ctx", None),
        P("tp"),
        P(("ctx", "seq"), None, "tp", None),
        P(("ctx", "seq"), None, "tp", None),
        P(("ctx", "seq"), None, "tp"),
        P(("ctx", "seq"), None, "tp"),
    )
    return jax.shard_map(
        on_device, mesh=mesh, in_specs=placed, out_specs=P("seq", "ctx", "tp"), check_vma=False
    )
```

```python
import functools

import jax
import jax.numpy as jnp
from jax import lax
from jax.experimental import pallas as pl
from jax.experimental.pallas import tpu as pltpu
from jax.sharding import PartitionSpec as P

MESH = pl.DeviceIdType.MESH

QB = 128


EPSILON = 1e-05


def flip(index, offset, size):
    total, bit = 0, 1
    while bit < size:
        total = total + bit * ((index // bit + offset // bit) % 2)
        bit *= 2
    return total


def layer_kernel(
    sizes,
    value_ref,
    gating_ref,
    write_ref,
    read_ref,
    step_ref,
    decay_ref,
    skip_ref,
    norm_gain_ref,
    out_weight_hbm,
    residual_ref,
    layer_gain_ref,
    routes_ref,
    route_weight_ref,
    gate_up_hbm,
    gate_up_scale_ref,
    down_hbm,
    down_scale_ref,
    stream_ref,
    mixed_ref,
    out_weight_ref,
    gate_up_ref,
    down_ref,
    fetch_sem,
    contrib,
    state_in,
    state_out,
    rows_in,
    product,
    mixed_out,
    mixed_in,
    square_out,
    square_in,
    state_send,
    state_recv,
    rows_send,
    rows_recv,
    mixed_send,
    mixed_recv,
    square_send,
    square_recv,
    high_slots,
    low_slots,
    high_rows,
    low_rows,
    slots,
    w_gate_up,
    w_down,
    received,
    partial_out,
    partial_in,
    hidden,
    answers,
    returned,
    row_send,
    row_recv,
    part_send,
    part_recv,
    hid_send,
    hid_recv,
    ans_send,
    ans_recv,
):
    n_ctx, n_seq, n_tp = sizes
    ctx, seq, tp = lax.axis_index("ctx"), lax.axis_index("seq"), lax.axis_index("tp")
    tokens, channels = value_ref.shape
    heads = step_ref.shape[0]
    groups, span = rows_in.shape[0], rows_in.shape[3]
    head_width = channels // heads
    per_group = heads // groups
    state_width = write_ref.shape[1] // groups
    columns, features = out_weight_ref.shape[1], residual_ref.shape[1]
    owners = features // columns
    pair = 2 * head_width
    f32, bf16 = jnp.float32, jnp.bfloat16

    def state_copy(g, target):
        return pltpu.make_async_remote_copy(
            src_ref=state_out.at[g],
            dst_ref=state_in.at[g],
            send_sem=state_send.at[g],
            recv_sem=state_recv.at[g],
            device_id={"ctx": target},
            device_id_type=MESH,
        )

    def rows_copy(g, source, slot, offset):
        return pltpu.make_async_remote_copy(
            src_ref=rows_in.at[g, source],
            dst_ref=rows_in.at[g, slot],
            send_sem=rows_send.at[g * n_ctx + slot],
            recv_sem=rows_recv.at[g * n_ctx + slot],
            device_id={"ctx": flip(ctx, offset, n_ctx)},
            device_id_type=MESH,
        )

    target_tp = ctx // owners

    def mixed_copy(a, slot):
        return pltpu.make_async_remote_copy(
            src_ref=mixed_out.at[a],
            dst_ref=mixed_in.at[slot],
            send_sem=mixed_send.at[a],
            recv_sem=mixed_recv.at[slot],
            device_id={"ctx": flip(ctx, a, n_ctx), "tp": target_tp},
            device_id_type=MESH,
        )

    def square_copy(i):
        return pltpu.make_async_remote_copy(
            src_ref=square_out,
            dst_ref=square_in.at[i - 1],
            send_sem=square_send.at[i - 1],
            recv_sem=square_recv.at[i - 1],
            device_id={"tp": lax.rem(tp + i, n_tp)},
            device_id_type=MESH,
        )

    barrier = pltpu.get_barrier_semaphore()
    for a in range(n_ctx):
        for i in range(n_tp):
            if a + i > 0:
                pl.semaphore_signal(
                    barrier,
                    inc=1,
                    device_id={"ctx": flip(ctx, a, n_ctx), "tp": lax.rem(tp + i, n_tp)},
                    device_id_type=MESH,
                )

    @pl.loop(n_ctx, n_ctx * n_seq)
    def _(r):
        pl.semaphore_signal(
            barrier,
            inc=1,
            device_id={"ctx": flip(ctx, r % n_ctx, n_ctx), "seq": flip(seq, r // n_ctx, n_seq)},
            device_id_type=MESH,
        )

    fetches = [
        pltpu.make_async_copy(source, target, fetch_sem.at[k])
        for k, (source, target) in enumerate(
            ((out_weight_hbm, out_weight_ref), (gate_up_hbm, gate_up_ref), (down_hbm, down_ref))
        )
    ]
    for fetch in fetches:
        fetch.start()

    step = step_ref[...]
    stride_t = jnp.maximum(step, 0.0) + jnp.log1p(jnp.exp(-jnp.abs(step)))
    stride = stride_t.T
    at_row = lax.broadcasted_iota(jnp.int32, (tokens, tokens), 0)
    at_col = lax.broadcasted_iota(jnp.int32, (tokens, tokens), 1)
    causal = at_row >= at_col
    cumul = jnp.dot(
        causal.astype(f32), stride * -jnp.exp(decay_ref[...]), precision=lax.Precision.HIGHEST
    )
    cumul_t = cumul.T
    final = cumul[tokens - 1 : tokens, :]
    coefficient = jnp.exp(final - cumul) * stride
    keep = jnp.exp(final)
    growth = jnp.exp(cumul)
    first_half = lax.broadcasted_iota(jnp.int32, (tokens, pair), 1) < head_width

    def widen(table, g):
        return jnp.concatenate(
            [
                jnp.where(first_half, table[:, h : h + 1], table[:, h + 1 : h + 2])
                for h in range(g * per_group, (g + 1) * per_group, 2)
            ],
            axis=1,
        )

    for g in range(groups):
        lanes = slice(g * span, (g + 1) * span)
        weighted = (value_ref[:, lanes].astype(f32) * widen(coefficient, g)).astype(bf16)
        contrib[g] = lax.dot_general(
            weighted,
            write_ref[:, g * state_width : (g + 1) * state_width],
            (((0,), (0,)), ((), ())),
            preferred_element_type=f32,
        )

    pl.semaphore_wait(barrier, n_ctx * (n_tp + n_seq - 1) - 1)

    @pl.when(ctx == 0)
    def _():
        state_in[...] = jnp.zeros_like(state_in)

    for g in range(groups):
        lanes = slice(g * span, (g + 1) * span)
        narrow = slice(g * state_width, (g + 1) * state_width)
        values = value_ref[:, lanes]
        scores = lax.dot_general(
            read_ref[:, narrow],
            write_ref[:, narrow],
            (((1,), (1,)), ((), ())),
            preferred_element_type=f32,
        )
        local = []
        for k in range(per_group // 2):
            block = values[:, k * pair : (k + 1) * pair]
            mixing = []
            for h in (g * per_group + 2 * k, g * per_group + 2 * k + 1):
                spread = cumul[:, h : h + 1] - cumul_t[h : h + 1, :]
                decay = jnp.exp(jnp.where(causal, spread, -jnp.inf)) * stride_t[h : h + 1, :]
                mixing.append((scores * decay).astype(bf16))
            zero = jnp.zeros_like(block)
            local.append(
                jnp.dot(
                    jnp.concatenate(mixing, axis=1),
                    jnp.concatenate(
                        [jnp.where(first_half, block, zero), jnp.where(first_half, zero, block)],
                        axis=0,
                    ),
                    preferred_element_type=f32,
                )
            )

        @pl.when(ctx > 0)
        def _():
            state_copy(g, ctx - 1).wait_recv()

        @pl.when(ctx < n_ctx - 1)
        def _():
            for j in range(per_group):
                h = g * per_group + j
                part = slice(j * head_width, (j + 1) * head_width)
                state_out[g, part, :] = (
                    state_in[g, part, :].astype(f32) * keep[:, h : h + 1] + contrib[g, part, :]
                ).astype(bf16)
            state_copy(g, ctx + 1).start()

        carried = lax.dot_general(
            read_ref[:, narrow],
            state_in[g],
            (((1,), (1,)), ((), ())),
            preferred_element_type=f32,
        )
        skip = jnp.concatenate(
            [
                jnp.where(first_half, skip_ref[h], skip_ref[h + 1])
                for h in range(g * per_group, (g + 1) * per_group, 2)
            ],
            axis=1,
        )
        output = (
            jnp.concatenate(local, axis=1)
            + widen(growth, g) * carried
            + skip * values.astype(f32)
        )
        gate = gating_ref[:, lanes].astype(f32)
        gated = output * (gate / (1.0 + jnp.exp(-gate)))
        scale = lax.rsqrt(jnp.mean(gated * gated, axis=1, keepdims=True) + EPSILON)
        rows_in[g, 0] = (gated * scale * norm_gain_ref[:, lanes]).astype(bf16)
        for a in range(2, n_ctx, 2):
            rows_copy(g, 0, a, a).start()
        rows_copy(g, 0, 1, 1).start()

    experts, capacity, feature_width = slots.shape
    half_width = w_down.shape[0]
    sources = n_ctx * n_seq
    ticks = lax.broadcasted_iota(jnp.int32, (experts, tokens), 0)
    named = [(ticks == routes_ref[k : k + 1, :]).astype(f32) for k in range(2)]
    earlier = jnp.dot(
        (named[0] + named[1]).astype(bf16),
        (at_row < at_col).astype(bf16),
        preferred_element_type=f32,
    )
    place = lax.broadcasted_iota(jnp.int32, (experts * capacity, tokens), 0)
    picker = jnp.zeros((experts * capacity, tokens), f32)
    weights = jnp.zeros((experts * capacity, tokens), f32)
    for k in range(2):
        rank = jnp.sum(named[k] * earlier, axis=0, keepdims=True).astype(jnp.int32)
        hit = place == routes_ref[k : k + 1, :] * capacity + rank
        picker = jnp.where(hit, 1.0, picker)
        weights = jnp.where(hit, route_weight_ref[k : k + 1, :], weights)
    picker = picker.astype(bf16)
    high = weights.astype(bf16)
    low = (weights - high.astype(f32)).astype(bf16)
    high_slots[...] = high.reshape(experts, capacity, tokens)
    low_slots[...] = low.reshape(experts, capacity, tokens)

    @pl.loop(0, sources)
    def _(r):
        holder = flip(ctx, r % n_ctx, n_ctx) * n_seq + flip(seq, r // n_ctx, n_seq)
        high_rows[r] = high_slots[holder // 2]
        low_rows[r] = low_slots[holder // 2]

    fetches[0].wait()

    def multiply(g):
        for a in range(1, n_ctx, 2):
            rows_copy(g, 0, a, a).wait_recv()
        part = jnp.dot(
            rows_in[g].reshape(n_ctx * tokens, span),
            out_weight_ref[g * span : (g + 1) * span, :],
            preferred_element_type=f32,
        )
        if g > 0:
            part = part + product[...]
        if g < groups - 1:
            product[...] = part
        else:
            mixed_out[...] = part.astype(bf16).reshape(n_ctx, tokens, columns)

    for g in range(groups):
        for a in range(2, n_ctx, 2):
            rows_copy(g, 0, a, a).wait_recv()
            rows_copy(g, a, a + 1, 1).start()
        if g > 0:
            multiply(g - 1)
    multiply(groups - 1)

    own_slot = lax.rem(ctx, owners) * n_tp + tp
    for a in range(1, n_ctx):
        mixed_copy(a, own_slot).start()

    @pl.when(tp == target_tp)
    def _():
        mixed_in[own_slot] = mixed_out[0]

    @pl.when(tp != target_tp)
    def _():
        mixed_copy(0, own_slot).start()

    squares = jnp.zeros((tokens, 1), f32)
    for q in range(owners):
        lanes = slice(q * columns, (q + 1) * columns)
        total = residual_ref[:, lanes].astype(f32)
        for i in range(n_tp):

            @pl.when((ctx != tp * owners + q) | (tp != i))
            def _():
                mixed_copy(1, q * n_tp + i).wait_recv()

            total = total + mixed_in[q * n_tp + i].astype(f32)
        total = total.astype(bf16)
        stream_ref[:, lanes] = total
        total = total.astype(f32)
        squares = squares + jnp.sum(total * total, axis=1, keepdims=True)
    across = jnp.broadcast_to(squares, (tokens, tokens)).T[:8]
    square_out[...] = across
    for i in range(1, n_tp):
        square_copy(i).start()
    for i in range(1, n_tp):
        square_copy(i).wait_recv()
        across = across + square_in[i - 1]
    squares = jnp.broadcast_to(across[:1], (tokens, tokens)).T[:, :1]
    scale = lax.rsqrt(squares / (features * n_tp) + EPSILON)
    expert_in = (stream_ref[...].astype(f32) * scale * layer_gain_ref[...]).astype(bf16)
    slots[...] = (
        jnp.dot(picker, expert_in, preferred_element_type=f32)
        .astype(bf16)
        .reshape(experts, capacity, feature_width)
    )

    teams = sources // n_tp

    def at_offset(r):
        return flip(ctx, r % n_ctx, n_ctx), flip(seq, r // n_ctx, n_seq)

    def row_copy(r):
        c, s = at_offset(r)
        return pltpu.make_async_remote_copy(
            src_ref=slots.at[(c * n_seq + s) // 2],
            dst_ref=received.at[r],
            send_sem=row_send.at[r],
            recv_sem=row_recv.at[r],
            device_id={"ctx": c, "seq": s},
            device_id_type=MESH,
        )

    def part_copy(g, i):
        peer = lax.rem(tp + i, n_tp)
        return pltpu.make_async_remote_copy(
            src_ref=partial_out.at[g * n_tp + peer],
            dst_ref=partial_in.at[g * (n_tp - 1) + i - 1],
            send_sem=part_send.at[g * (n_tp - 1) + i - 1],
            recv_sem=part_recv.at[g * (n_tp - 1) + i - 1],
            device_id={"tp": peer},
            device_id_type=MESH,
        )

    def hid_copy(g, i):
        peer = lax.rem(tp + i, n_tp)
        return pltpu.make_async_remote_copy(
            src_ref=hidden.at[g * n_tp + tp],
            dst_ref=hidden.at[g * n_tp + tp],
            send_sem=hid_send.at[g * (n_tp - 1) + i - 1],
            recv_sem=hid_recv.at[g * (n_tp - 1) + i - 1],
            device_id={"tp": peer},
            device_id_type=MESH,
        )

    def hid_arrival(g, i):
        origin = lax.rem(tp + n_tp - i, n_tp)
        return pltpu.make_async_remote_copy(
            src_ref=hidden.at[g * n_tp + origin],
            dst_ref=hidden.at[g * n_tp + origin],
            send_sem=hid_send.at[g * (n_tp - 1) + i - 1],
            recv_sem=hid_recv.at[g * (n_tp - 1) + i - 1],
            device_id={"tp": origin},
            device_id_type=MESH,
        )

    def ans_copy(r):
        c, s = at_offset(r)
        return pltpu.make_async_remote_copy(
            src_ref=answers.at[r],
            dst_ref=returned.at[r],
            send_sem=ans_send.at[r],
            recv_sem=ans_recv.at[r],
            device_id={"ctx": c, "seq": s},
            device_id_type=MESH,
        )

    @pl.loop(1, sources)
    def _(r):
        row_copy(r).start()

    received[0] = slots[(ctx * n_seq + seq) // 2]
    fetches[1].wait()
    fetches[2].wait()

    @pl.loop(0, feature_width // QB)
    def _(i):
        rows = pl.ds(pl.multiple_of(i * QB, QB), QB)
        for kind in range(2):
            for j in range(half_width // QB):
                w_gate_up[rows, kind * half_width + j * QB : kind * half_width + (j + 1) * QB] = (
                    gate_up_ref[kind, rows, j * QB : (j + 1) * QB].astype(jnp.float32)
                    * gate_up_scale_ref[kind, i, j]
                ).astype(jnp.bfloat16)

    @pl.loop(0, half_width // QB)
    def _(i):
        rows = pl.ds(pl.multiple_of(i * QB, QB), QB)
        for j in range(feature_width // QB):
            w_down[rows, j * QB : (j + 1) * QB] = (
                down_ref[rows, j * QB : (j + 1) * QB].astype(jnp.float32) * down_scale_ref[i, j]
            ).astype(jnp.bfloat16)

    @pl.loop(0, teams + 2)
    def _(step):
        @pl.when(step < teams)
        def _():
            g = step
            for i in range(n_tp):
                r = g * n_tp + i
                if i == 0:

                    @pl.when(g > 0)
                    def _():
                        row_copy(r).wait_recv()
                else:
                    row_copy(r).wait_recv()
            rows = received[pl.ds(g * n_tp, n_tp)].reshape(n_tp * capacity, feature_width)
            both = jnp.dot(rows, w_gate_up[...], preferred_element_type=jnp.float32)
            partial_out[pl.ds(g * n_tp, n_tp)] = both.astype(jnp.bfloat16).reshape(
                n_tp, capacity, 2 * half_width
            )
            for i in range(1, n_tp):
                part_copy(g, i).start()

        @pl.when((step >= 1) & (step < teams + 1))
        def _():
            g = step - 1
            total = partial_out[g * n_tp + tp].astype(jnp.float32)
            for i in range(1, n_tp):
                part_copy(g, i).wait_recv()
                total = total + partial_in[g * (n_tp - 1) + i - 1].astype(jnp.float32)
            gate, up = total[:, :half_width], total[:, half_width:]
            hidden[g * n_tp + tp] = (gate / (1.0 + jnp.exp(-gate)) * up).astype(jnp.bfloat16)
            for i in range(1, n_tp):
                hid_copy(g, i).start()

        @pl.when(step >= 2)
        def _():
            g = step - 2
            for i in range(1, n_tp):
                hid_arrival(g, i).wait_recv()
            rows = hidden[pl.ds(g * n_tp, n_tp)].reshape(n_tp * capacity, half_width)
            answer = jnp.dot(rows, w_down[...], preferred_element_type=jnp.float32)
            answers[pl.ds(g * n_tp, n_tp)] = answer.astype(jnp.bfloat16).reshape(
                n_tp, capacity, feature_width
            )
            for i in range(n_tp):
                r = g * n_tp + i
                if i == 0:

                    @pl.when(g > 0)
                    def _():
                        ans_copy(r).start()
                else:
                    ans_copy(r).start()

    returned[0] = answers[0]

    @pl.loop(1, sources)
    def _(r):
        ans_copy(r).wait_recv()

    back = returned[...].reshape(sources * capacity, feature_width)
    contract = (((0,), (0,)), ((), ()))
    mixed = 0.0
    for rows in (high_rows, low_rows):
        mixed = mixed + lax.dot_general(
            rows[...].reshape(sources * capacity, tokens),
            back,
            contract,
            preferred_element_type=f32,
        )
    mixed_ref[...] = mixed

    @pl.loop(1, sources)
    def _(r):
        row_copy(r).wait_send()
        ans_copy(r).wait_send()

    @pl.loop(0, teams)
    def _(g):
        for i in range(1, n_tp):
            part_copy(g, i).wait_send()
            hid_copy(g, i).wait_send()

    for i in range(1, n_tp):
        square_copy(i).wait_send()
    for a in range(1, n_ctx):
        mixed_copy(a, own_slot).wait_send()

    @pl.when(tp != target_tp)
    def _():
        mixed_copy(0, own_slot).wait_send()

    for g in range(groups):
        for a in range(1, n_ctx):
            rows_copy(g, 0, a, a).wait_send()

    @pl.when(ctx < n_ctx - 1)
    def _():
        for g in range(groups):
            state_copy(g, ctx + 1).wait_send()


def both_layers(
    values,
    gating,
    writes,
    reads,
    step,
    decay,
    skip,
    norm_gain,
    out_weight,
    residual,
    layer_gain,
    routes,
    route_weight,
    gate_up,
    gate_up_scale,
    down,
    down_scale,
):
    sizes = tuple(lax.axis_size(axis) for axis in ("ctx", "seq", "tp"))
    n_ctx, n_seq, n_tp = sizes
    tokens, channels = values.shape
    groups, state_width = writes.shape[1], writes.shape[2]
    span = channels // groups
    columns, features = out_weight.shape[1], residual.shape[1]
    sources = n_ctx * n_seq
    experts = sources // 2
    capacity = -(-(3 * tokens // experts) // 16) * 16
    half_width = down.shape[0]
    shares = sources // n_tp * (n_tp - 1)
    slots = features // columns * n_tp
    dma = pltpu.SemaphoreType.DMA
    vmem, smem = pl.BlockSpec(memory_space=pltpu.VMEM), pl.BlockSpec(memory_space=pltpu.SMEM)
    hbm = pl.BlockSpec(memory_space=pl.ANY)

    def wide(*shape):
        return pltpu.VMEM(shape, jnp.float32)

    def half(*shape):
        return pltpu.VMEM(shape, jnp.bfloat16)

    stream, mixed = pl.pallas_call(
        functools.partial(layer_kernel, sizes),
        out_shape=(
            jax.ShapeDtypeStruct((tokens, features), jnp.bfloat16),
            jax.ShapeDtypeStruct((tokens, features), jnp.float32),
        ),
        in_specs=[vmem] * 6
        + [smem, vmem, hbm, vmem, vmem, vmem, vmem]
        + [hbm, smem, hbm, smem],
        out_specs=(vmem, vmem),
        scratch_shapes=[
            half(*out_weight.shape),
            half(*gate_up.shape),
            half(*down.shape),
            dma((3,)),
            wide(groups, span, state_width),
            half(groups, span, state_width),
            half(groups, span, state_width),
            half(groups, n_ctx, tokens, span),
            wide(n_ctx * tokens, columns),
            half(n_ctx, tokens, columns),
            half(slots, tokens, columns),
            wide(8, tokens),
            wide(n_tp - 1, 8, tokens),
            dma((groups,)),
            dma((groups,)),
            dma((groups * n_ctx,)),
            dma((groups * n_ctx,)),
            dma((n_ctx,)),
            dma((slots,)),
            dma((n_tp - 1,)),
            dma((n_tp - 1,)),
            half(experts, capacity, tokens),
            half(experts, capacity, tokens),
            half(sources, capacity, tokens),
            half(sources, capacity, tokens),
            half(experts, capacity, features),
            half(features, 2 * half_width),
            half(half_width, features),
            half(sources, capacity, features),
            half(sources, capacity, 2 * half_width),
            half(shares, capacity, 2 * half_width),
            half(sources, capacity, half_width),
            half(sources, capacity, features),
            half(sources, capacity, features),
            dma((sources,)),
            dma((sources,)),
            dma((shares,)),
            dma((shares,)),
            dma((shares,)),
            dma((shares,)),
            dma((sources,)),
            dma((sources,)),
        ],
        compiler_params=pltpu.CompilerParams(
            collective_id=1, has_side_effects=True, vmem_limit_bytes=60 * 1024 * 1024
        ),
    )(
        values,
        gating,
        writes.reshape(tokens, groups * state_width),
        reads.reshape(tokens, groups * state_width),
        step.T,
        decay[None],
        skip,
        norm_gain[None],
        out_weight,
        residual,
        layer_gain[None],
        routes.T,
        route_weight.T,
        gate_up,
        gate_up_scale,
        down,
        down_scale,
    )
    return (stream.astype(jnp.float32) + mixed).astype(jnp.bfloat16)


def on_device(
    inputs,
    gating,
    write_proj,
    read_proj,
    step_raw,
    decay_log,
    skip_gain,
    norm_gain,
    out_weight,
    residual,
    routes,
    route_weight,
    layer_gain,
    gate_up_codes,
    gate_up_scales,
    down_codes,
    down_scales,
):
    return both_layers(
        inputs[0],
        gating[0],
        write_proj[0],
        read_proj[0],
        step_raw[0],
        decay_log,
        skip_gain,
        norm_gain,
        out_weight,
        residual[0],
        layer_gain,
        routes[0],
        route_weight[0],
        gate_up_codes[0],
        gate_up_scales[0],
        down_codes[0],
        down_scales[0],
    )[None]


def solution(mesh):
    placed = (
        P("seq", "ctx", "tp"),
        P("seq", "ctx", "tp"),
        P("seq", "ctx", "tp", None),
        P("seq", "ctx", "tp", None),
        P("seq", "ctx", "tp"),
        P("tp"),
        P("tp"),
        P("tp"),
        P("tp", "ctx"),
        P("seq", "ctx", "tp"),
        P("seq", "ctx", None),
        P("seq", "ctx", None),
        P("tp"),
        P(("ctx", "seq"), None, "tp", None),
        P(("ctx", "seq"), None, "tp", None),
        P(("ctx", "seq"), None, "tp"),
        P(("ctx", "seq"), None, "tp"),
    )
    return jax.shard_map(
        on_device, mesh=mesh, in_specs=placed, out_specs=P("seq", "ctx", "tp"), check_vma=False
    )
```

```python
import functools

import jax
import jax.numpy as jnp
from jax import lax
from jax.experimental import pallas as pl
from jax.experimental.pallas import tpu as pltpu
from jax.sharding import PartitionSpec as P

MESH = pl.DeviceIdType.MESH

QB = 128


EPSILON = 1e-05


def flip(index, offset, size):
    total, bit = 0, 1
    while bit < size:
        total = total + bit * ((index // bit + offset // bit) % 2)
        bit *= 2
    return total


def layer_kernel(
    sizes,
    value_ref,
    gating_ref,
    write_ref,
    read_ref,
    step_ref,
    decay_ref,
    skip_ref,
    norm_gain_ref,
    out_weight_hbm,
    residual_ref,
    layer_gain_ref,
    routes_ref,
    route_weight_ref,
    gate_up_hbm,
    gate_up_scale_ref,
    down_hbm,
    down_scale_ref,
    stream_ref,
    mixed_ref,
    out_weight_ref,
    gate_up_ref,
    down_ref,
    fetch_sem,
    contrib,
    state_in,
    state_out,
    rows_in,
    product,
    mixed_out,
    mixed_in,
    square_out,
    square_in,
    state_send,
    state_recv,
    rows_send,
    rows_recv,
    mixed_send,
    mixed_recv,
    square_send,
    square_recv,
    high_slots,
    low_slots,
    high_rows,
    low_rows,
    slots,
    w_gate_up,
    w_down,
    received,
    partial_out,
    partial_in,
    hidden,
    answers,
    returned,
    row_send,
    row_recv,
    part_send,
    part_recv,
    hid_send,
    hid_recv,
    ans_send,
    ans_recv,
    half_in,
    half_recv,
):
    n_ctx, n_seq, n_tp = sizes
    ctx, seq, tp = lax.axis_index("ctx"), lax.axis_index("seq"), lax.axis_index("tp")
    tokens, channels = value_ref.shape
    heads = step_ref.shape[0]
    groups, span = rows_in.shape[0], rows_in.shape[3]
    head_width = channels // heads
    per_group = heads // groups
    state_width = write_ref.shape[1] // groups
    columns, features = out_weight_ref.shape[1], residual_ref.shape[1]
    owners = features // columns
    pair = 2 * head_width
    f32, bf16 = jnp.float32, jnp.bfloat16

    def state_copy(g, target):
        return pltpu.make_async_remote_copy(
            src_ref=state_out.at[g],
            dst_ref=state_in.at[g],
            send_sem=state_send.at[g],
            recv_sem=state_recv.at[g],
            device_id={"ctx": target},
            device_id_type=MESH,
        )

    def rows_copy(g, source, slot, offset):
        return pltpu.make_async_remote_copy(
            src_ref=rows_in.at[g, source],
            dst_ref=rows_in.at[g, slot],
            send_sem=rows_send.at[g * n_ctx + slot],
            recv_sem=rows_recv.at[g * n_ctx + slot],
            device_id={"ctx": flip(ctx, offset, n_ctx)},
            device_id_type=MESH,
        )

    target_tp = ctx // owners

    def mixed_copy(a, slot):
        return pltpu.make_async_remote_copy(
            src_ref=mixed_out.at[a],
            dst_ref=mixed_in.at[slot],
            send_sem=mixed_send.at[a],
            recv_sem=mixed_recv.at[slot],
            device_id={"ctx": flip(ctx, a, n_ctx), "tp": target_tp},
            device_id_type=MESH,
        )

    def square_copy(i):
        return pltpu.make_async_remote_copy(
            src_ref=square_out,
            dst_ref=square_in.at[i - 1],
            send_sem=square_send.at[i - 1],
            recv_sem=square_recv.at[i - 1],
            device_id={"tp": lax.rem(tp + i, n_tp)},
            device_id_type=MESH,
        )

    barrier = pltpu.get_barrier_semaphore()
    for a in range(n_ctx):
        for i in range(n_tp):
            if a + i > 0:
                pl.semaphore_signal(
                    barrier,
                    inc=1,
                    device_id={"ctx": flip(ctx, a, n_ctx), "tp": lax.rem(tp + i, n_tp)},
                    device_id_type=MESH,
                )

    @pl.loop(n_ctx, n_ctx * n_seq)
    def _(r):
        pl.semaphore_signal(
            barrier,
            inc=1,
            device_id={"ctx": flip(ctx, r % n_ctx, n_ctx), "seq": flip(seq, r // n_ctx, n_seq)},
            device_id_type=MESH,
        )

    fetches = [
        pltpu.make_async_copy(source, target, fetch_sem.at[k])
        for k, (source, target) in enumerate(
            ((out_weight_hbm, out_weight_ref), (gate_up_hbm, gate_up_ref), (down_hbm, down_ref))
        )
    ]
    for fetch in fetches:
        fetch.start()

    step = step_ref[...]
    stride_t = jnp.maximum(step, 0.0) + jnp.log1p(jnp.exp(-jnp.abs(step)))
    stride = stride_t.T
    at_row = lax.broadcasted_iota(jnp.int32, (tokens, tokens), 0)
    at_col = lax.broadcasted_iota(jnp.int32, (tokens, tokens), 1)
    causal = at_row >= at_col
    cumul = jnp.dot(
        causal.astype(f32), stride * -jnp.exp(decay_ref[...]), precision=lax.Precision.HIGHEST
    )
    cumul_t = cumul.T
    final = cumul[tokens - 1 : tokens, :]
    coefficient = jnp.exp(final - cumul) * stride
    keep = jnp.exp(final)
    growth = jnp.exp(cumul)
    first_half = lax.broadcasted_iota(jnp.int32, (tokens, pair), 1) < head_width

    def widen(table, g):
        return jnp.concatenate(
            [
                jnp.where(first_half, table[:, h : h + 1], table[:, h + 1 : h + 2])
                for h in range(g * per_group, (g + 1) * per_group, 2)
            ],
            axis=1,
        )

    for g in range(groups):
        lanes = slice(g * span, (g + 1) * span)
        weighted = (value_ref[:, lanes].astype(f32) * widen(coefficient, g)).astype(bf16)
        contrib[g] = lax.dot_general(
            weighted,
            write_ref[:, g * state_width : (g + 1) * state_width],
            (((0,), (0,)), ((), ())),
            preferred_element_type=f32,
        )

    pl.semaphore_wait(barrier, n_ctx * (n_tp + n_seq - 1) - 1)

    @pl.when(ctx == 0)
    def _():
        state_in[...] = jnp.zeros_like(state_in)

    for g in range(groups):
        lanes = slice(g * span, (g + 1) * span)
        narrow = slice(g * state_width, (g + 1) * state_width)
        values = value_ref[:, lanes]
        scores = lax.dot_general(
            read_ref[:, narrow],
            write_ref[:, narrow],
            (((1,), (1,)), ((), ())),
            preferred_element_type=f32,
        )
        local = []
        for k in range(per_group // 2):
            block = values[:, k * pair : (k + 1) * pair]
            mixing = []
            for h in (g * per_group + 2 * k, g * per_group + 2 * k + 1):
                spread = cumul[:, h : h + 1] - cumul_t[h : h + 1, :]
                decay = jnp.exp(jnp.where(causal, spread, -jnp.inf)) * stride_t[h : h + 1, :]
                mixing.append((scores * decay).astype(bf16))
            zero = jnp.zeros_like(block)
            local.append(
                jnp.dot(
                    jnp.concatenate(mixing, axis=1),
                    jnp.concatenate(
                        [jnp.where(first_half, block, zero), jnp.where(first_half, zero, block)],
                        axis=0,
                    ),
                    preferred_element_type=f32,
                )
            )

        @pl.when(ctx > 0)
        def _():
            state_copy(g, ctx - 1).wait_recv()

        @pl.when(ctx < n_ctx - 1)
        def _():
            for j in range(per_group):
                h = g * per_group + j
                part = slice(j * head_width, (j + 1) * head_width)
                state_out[g, part, :] = (
                    state_in[g, part, :].astype(f32) * keep[:, h : h + 1] + contrib[g, part, :]
                ).astype(bf16)
            state_copy(g, ctx + 1).start()

        carried = lax.dot_general(
            read_ref[:, narrow],
            state_in[g],
            (((1,), (1,)), ((), ())),
            preferred_element_type=f32,
        )
        skip = jnp.concatenate(
            [
                jnp.where(first_half, skip_ref[h], skip_ref[h + 1])
                for h in range(g * per_group, (g + 1) * per_group, 2)
            ],
            axis=1,
        )
        output = (
            jnp.concatenate(local, axis=1)
            + widen(growth, g) * carried
            + skip * values.astype(f32)
        )
        gate = gating_ref[:, lanes].astype(f32)
        gated = output * (gate / (1.0 + jnp.exp(-gate)))
        scale = lax.rsqrt(jnp.mean(gated * gated, axis=1, keepdims=True) + EPSILON)
        rows_in[g, 0] = (gated * scale * norm_gain_ref[:, lanes]).astype(bf16)
        for a in range(2, n_ctx, 2):
            rows_copy(g, 0, a, a).start()
        rows_copy(g, 0, 1, 1).start()

    experts, capacity, feature_width = slots.shape
    half_width = w_down.shape[0]
    sources = n_ctx * n_seq
    ticks = lax.broadcasted_iota(jnp.int32, (experts, tokens), 0)
    named = [(ticks == routes_ref[k : k + 1, :]).astype(f32) for k in range(2)]
    earlier = jnp.dot(
        (named[0] + named[1]).astype(bf16),
        (at_row < at_col).astype(bf16),
        preferred_element_type=f32,
    )
    place = lax.broadcasted_iota(jnp.int32, (experts * capacity, tokens), 0)
    picker = jnp.zeros((experts * capacity, tokens), f32)
    weights = jnp.zeros((experts * capacity, tokens), f32)
    for k in range(2):
        rank = jnp.sum(named[k] * earlier, axis=0, keepdims=True).astype(jnp.int32)
        hit = place == routes_ref[k : k + 1, :] * capacity + rank
        picker = jnp.where(hit, 1.0, picker)
        weights = jnp.where(hit, route_weight_ref[k : k + 1, :], weights)
    picker = picker.astype(bf16)
    high = weights.astype(bf16)
    low = (weights - high.astype(f32)).astype(bf16)
    high_slots[...] = high.reshape(experts, capacity, tokens)
    low_slots[...] = low.reshape(experts, capacity, tokens)

    @pl.loop(0, experts)
    def _(q):
        holder = flip(ctx, q % n_ctx, n_ctx) * n_seq + flip(seq, q // n_ctx * 2, n_seq)
        high_rows[q] = high_slots[holder // 2]
        low_rows[q] = low_slots[holder // 2]

    fetches[0].wait()

    def multiply(g):
        for a in range(1, n_ctx, 2):
            rows_copy(g, 0, a, a).wait_recv()
        part = jnp.dot(
            rows_in[g].reshape(n_ctx * tokens, span),
            out_weight_ref[g * span : (g + 1) * span, :],
            preferred_element_type=f32,
        )
        if g > 0:
            part = part + product[...]
        if g < groups - 1:
            product[...] = part
        else:
            mixed_out[...] = part.astype(bf16).reshape(n_ctx, tokens, columns)

    for g in range(groups):
        for a in range(2, n_ctx, 2):
            rows_copy(g, 0, a, a).wait_recv()
            rows_copy(g, a, a + 1, 1).start()
        if g > 0:
            multiply(g - 1)
    multiply(groups - 1)

    own_slot = lax.rem(ctx, owners) * n_tp + tp
    for a in range(1, n_ctx):
        mixed_copy(a, own_slot).start()

    @pl.when(tp == target_tp)
    def _():
        mixed_in[own_slot] = mixed_out[0]

    @pl.when(tp != target_tp)
    def _():
        mixed_copy(0, own_slot).start()

    squares = jnp.zeros((tokens, 1), f32)
    for q in range(owners):
        lanes = slice(q * columns, (q + 1) * columns)
        total = residual_ref[:, lanes].astype(f32)
        for i in range(n_tp):

            @pl.when((ctx != tp * owners + q) | (tp != i))
            def _():
                mixed_copy(1, q * n_tp + i).wait_recv()

            total = total + mixed_in[q * n_tp + i].astype(f32)
        total = total.astype(bf16)
        stream_ref[:, lanes] = total
        total = total.astype(f32)
        squares = squares + jnp.sum(total * total, axis=1, keepdims=True)
    across = jnp.broadcast_to(squares, (tokens, tokens)).T[:8]
    square_out[...] = across
    for i in range(1, n_tp):
        square_copy(i).start()
    for i in range(1, n_tp):
        square_copy(i).wait_recv()
        across = across + square_in[i - 1]
    squares = jnp.broadcast_to(across[:1], (tokens, tokens)).T[:, :1]
    scale = lax.rsqrt(squares / (features * n_tp) + EPSILON)
    expert_in = (stream_ref[...].astype(f32) * scale * layer_gain_ref[...]).astype(bf16)
    slots[...] = (
        jnp.dot(picker, expert_in, preferred_element_type=f32)
        .astype(bf16)
        .reshape(experts, capacity, feature_width)
    )

    teams = sources // n_tp

    def at_offset(r):
        return flip(ctx, r % n_ctx, n_ctx), flip(seq, r // n_ctx, n_seq)

    def row_copy(r):
        c, s = at_offset(r)
        return pltpu.make_async_remote_copy(
            src_ref=slots.at[(c * n_seq + s) // 2],
            dst_ref=received.at[r],
            send_sem=row_send.at[r],
            recv_sem=row_recv.at[r],
            device_id={"ctx": c, "seq": s},
            device_id_type=MESH,
        )

    def part_copy(g, i):
        peer = lax.rem(tp + i, n_tp)
        return pltpu.make_async_remote_copy(
            src_ref=partial_out.at[g * n_tp + peer],
            dst_ref=partial_in.at[g * (n_tp - 1) + i - 1],
            send_sem=part_send.at[g * (n_tp - 1) + i - 1],
            recv_sem=part_recv.at[g * (n_tp - 1) + i - 1],
            device_id={"tp": peer},
            device_id_type=MESH,
        )

    def hid_copy(g, i):
        peer = lax.rem(tp + i, n_tp)
        return pltpu.make_async_remote_copy(
            src_ref=hidden.at[g * n_tp + tp],
            dst_ref=hidden.at[g * n_tp + tp],
            send_sem=hid_send.at[g * (n_tp - 1) + i - 1],
            recv_sem=hid_recv.at[g * (n_tp - 1) + i - 1],
            device_id={"tp": peer},
            device_id_type=MESH,
        )

    def hid_arrival(g, i):
        origin = lax.rem(tp + n_tp - i, n_tp)
        return pltpu.make_async_remote_copy(
            src_ref=hidden.at[g * n_tp + origin],
            dst_ref=hidden.at[g * n_tp + origin],
            send_sem=hid_send.at[g * (n_tp - 1) + i - 1],
            recv_sem=hid_recv.at[g * (n_tp - 1) + i - 1],
            device_id={"tp": origin},
            device_id_type=MESH,
        )

    def near(r):
        return (r // n_ctx) % 2 == 0

    def slot(r):
        return r // (2 * n_ctx) * n_ctx + r % n_ctx

    def forward_copy(r):
        return pltpu.make_async_remote_copy(
            src_ref=received.at[r],
            dst_ref=received.at[r + n_ctx],
            send_sem=row_send.at[r + n_ctx],
            recv_sem=row_recv.at[r + n_ctx],
            device_id={"seq": flip(seq, 1, n_seq)},
            device_id_type=MESH,
        )

    def half_copy(r):
        return pltpu.make_async_remote_copy(
            src_ref=answers.at[r],
            dst_ref=half_in.at[slot(r - n_ctx)],
            send_sem=ans_send.at[r],
            recv_sem=half_recv.at[slot(r - n_ctx)],
            device_id={"seq": flip(seq, 1, n_seq)},
            device_id_type=MESH,
        )

    def ans_copy(r):
        c, s = at_offset(r)
        return pltpu.make_async_remote_copy(
            src_ref=answers.at[r],
            dst_ref=returned.at[slot(r)],
            send_sem=ans_send.at[r],
            recv_sem=ans_recv.at[slot(r)],
            device_id={"ctx": c, "seq": s},
            device_id_type=MESH,
        )

    @pl.loop(1, sources)
    def _(r):
        @pl.when(near(r))
        def _():
            row_copy(r).start()

    received[0] = slots[(ctx * n_seq + seq) // 2]
    forward_copy(0).start()
    fetches[1].wait()
    fetches[2].wait()

    @pl.loop(0, feature_width // QB)
    def _(i):
        rows = pl.ds(pl.multiple_of(i * QB, QB), QB)
        for kind in range(2):
            for j in range(half_width // QB):
                w_gate_up[rows, kind * half_width + j * QB : kind * half_width + (j + 1) * QB] = (
                    gate_up_ref[kind, rows, j * QB : (j + 1) * QB].astype(jnp.float32)
                    * gate_up_scale_ref[kind, pl.ds(i, 1), j : j + 1]
                ).astype(jnp.bfloat16)

    @pl.loop(0, half_width // QB)
    def _(i):
        rows = pl.ds(pl.multiple_of(i * QB, QB), QB)
        for j in range(feature_width // QB):
            w_down[rows, j * QB : (j + 1) * QB] = (
                down_ref[rows, j * QB : (j + 1) * QB].astype(jnp.float32) * down_scale_ref[pl.ds(i, 1), j : j + 1]
            ).astype(jnp.bfloat16)

    delay = n_ctx // n_tp + 1

    @pl.loop(0, teams + 3)
    def _(step):
        @pl.when(step < teams)
        def _():
            g = step
            for i in range(n_tp):
                r = g * n_tp + i
                if i == 0:

                    @pl.when(g > 0)
                    def _():
                        row_copy(r).wait_recv()
                else:
                    row_copy(r).wait_recv()

                @pl.when(near(r) & (r > 0))
                def _():
                    forward_copy(r).start()
            rows = received[pl.ds(g * n_tp, n_tp)].reshape(n_tp * capacity, feature_width)
            both = jnp.dot(rows, w_gate_up[...], preferred_element_type=jnp.float32)
            partial_out[pl.ds(g * n_tp, n_tp)] = both.astype(jnp.bfloat16).reshape(
                n_tp, capacity, 2 * half_width
            )
            for i in range(1, n_tp):
                part_copy(g, i).start()

        @pl.when((step >= 1) & (step < teams + 1))
        def _():
            g = step - 1
            total = partial_out[g * n_tp + tp].astype(jnp.float32)
            for i in range(1, n_tp):
                part_copy(g, i).wait_recv()
                total = total + partial_in[g * (n_tp - 1) + i - 1].astype(jnp.float32)
            gate, up = total[:, :half_width], total[:, half_width:]
            hidden[g * n_tp + tp] = (gate / (1.0 + jnp.exp(-gate)) * up).astype(jnp.bfloat16)
            for i in range(1, n_tp):
                hid_copy(g, i).start()

        @pl.when((step >= 2) & (step < teams + 2))
        def _():
            g = step - 2
            for i in range(1, n_tp):
                hid_arrival(g, i).wait_recv()
            rows = hidden[pl.ds(g * n_tp, n_tp)].reshape(n_tp * capacity, half_width)
            answer = jnp.dot(rows, w_down[...], preferred_element_type=jnp.float32)
            answers[pl.ds(g * n_tp, n_tp)] = answer.astype(jnp.bfloat16).reshape(
                n_tp, capacity, feature_width
            )
            for i in range(n_tp):
                r = g * n_tp + i

                @pl.when((r // n_ctx) % 2 == 1)
                def _():
                    half_copy(r).start()

        @pl.when(step >= 2 + delay)
        def _():
            for i in range(n_tp):
                r = (step - 2 - delay) * n_tp + i

                @pl.when(near(r))
                def _():
                    half_copy(r + n_ctx).wait_recv()
                    answers[r] = (
                        answers[r].astype(jnp.float32) + half_in[slot(r)].astype(jnp.float32)
                    ).astype(jnp.bfloat16)

                    @pl.when(r > 0)
                    def _():
                        ans_copy(r).start()

    returned[0] = answers[0]

    @pl.loop(1, sources)
    def _(r):
        @pl.when(near(r))
        def _():
            ans_copy(r).wait_recv()

    back = returned[...].reshape(experts * capacity, feature_width)
    contract = (((0,), (0,)), ((), ()))
    mixed = 0.0
    for rows in (high_rows, low_rows):
        mixed = mixed + lax.dot_general(
            rows[...].reshape(experts * capacity, tokens),
            back,
            contract,
            preferred_element_type=f32,
        )
    mixed_ref[...] = mixed

    @pl.loop(1, sources)
    def _(r):
        row_copy(r).wait_send()
        pltpu.make_async_remote_copy(
            src_ref=answers.at[r],
            dst_ref=returned.at[0],
            send_sem=ans_send.at[r],
            recv_sem=ans_recv.at[0],
            device_id={"seq": flip(seq, 1, n_seq)},
            device_id_type=MESH,
        ).wait_send()

    @pl.loop(0, teams)
    def _(g):
        for i in range(1, n_tp):
            part_copy(g, i).wait_send()
            hid_copy(g, i).wait_send()

    for i in range(1, n_tp):
        square_copy(i).wait_send()
    for a in range(1, n_ctx):
        mixed_copy(a, own_slot).wait_send()

    @pl.when(tp != target_tp)
    def _():
        mixed_copy(0, own_slot).wait_send()

    for g in range(groups):
        for a in range(1, n_ctx):
            rows_copy(g, 0, a, a).wait_send()

    @pl.when(ctx < n_ctx - 1)
    def _():
        for g in range(groups):
            state_copy(g, ctx + 1).wait_send()


def both_layers(
    values,
    gating,
    writes,
    reads,
    step,
    decay,
    skip,
    norm_gain,
    out_weight,
    residual,
    layer_gain,
    routes,
    route_weight,
    gate_up,
    gate_up_scale,
    down,
    down_scale,
):
    sizes = tuple(lax.axis_size(axis) for axis in ("ctx", "seq", "tp"))
    n_ctx, n_seq, n_tp = sizes
    tokens, channels = values.shape
    groups, state_width = writes.shape[1], writes.shape[2]
    span = channels // groups
    columns, features = out_weight.shape[1], residual.shape[1]
    sources = n_ctx * n_seq
    experts = sources // 2
    capacity = -(-(3 * tokens // experts) // 16) * 16
    half_width = down.shape[0]
    shares = sources // n_tp * (n_tp - 1)
    slots = features // columns * n_tp
    dma = pltpu.SemaphoreType.DMA
    vmem, smem = pl.BlockSpec(memory_space=pltpu.VMEM), pl.BlockSpec(memory_space=pltpu.SMEM)
    hbm = pl.BlockSpec(memory_space=pl.ANY)

    def wide(*shape):
        return pltpu.VMEM(shape, jnp.float32)

    def half(*shape):
        return pltpu.VMEM(shape, jnp.bfloat16)

    stream, mixed = pl.pallas_call(
        functools.partial(layer_kernel, sizes),
        out_shape=(
            jax.ShapeDtypeStruct((tokens, features), jnp.bfloat16),
            jax.ShapeDtypeStruct((tokens, features), jnp.float32),
        ),
        in_specs=[vmem] * 6
        + [smem, vmem, hbm, vmem, vmem, vmem, vmem]
        + [hbm, vmem, hbm, vmem],
        out_specs=(vmem, vmem),
        scratch_shapes=[
            half(*out_weight.shape),
            half(*gate_up.shape),
            half(*down.shape),
            dma((3,)),
            wide(groups, span, state_width),
            half(groups, span, state_width),
            half(groups, span, state_width),
            half(groups, n_ctx, tokens, span),
            wide(n_ctx * tokens, columns),
            half(n_ctx, tokens, columns),
            half(slots, tokens, columns),
            wide(8, tokens),
            wide(n_tp - 1, 8, tokens),
            dma((groups,)),
            dma((groups,)),
            dma((groups * n_ctx,)),
            dma((groups * n_ctx,)),
            dma((n_ctx,)),
            dma((slots,)),
            dma((n_tp - 1,)),
            dma((n_tp - 1,)),
            half(experts, capacity, tokens),
            half(experts, capacity, tokens),
            half(experts, capacity, tokens),
            half(experts, capacity, tokens),
            half(experts, capacity, features),
            half(features, 2 * half_width),
            half(half_width, features),
            half(sources, capacity, features),
            half(sources, capacity, 2 * half_width),
            half(shares, capacity, 2 * half_width),
            half(sources, capacity, half_width),
            half(sources, capacity, features),
            half(experts, capacity, features),
            dma((sources,)),
            dma((sources,)),
            dma((shares,)),
            dma((shares,)),
            dma((shares,)),
            dma((shares,)),
            dma((sources,)),
            dma((experts,)),
            half(experts, capacity, features),
            dma((experts,)),
        ],
        compiler_params=pltpu.CompilerParams(
            collective_id=1, has_side_effects=True, vmem_limit_bytes=60 * 1024 * 1024
        ),
    )(
        values,
        gating,
        writes.reshape(tokens, groups * state_width),
        reads.reshape(tokens, groups * state_width),
        step.T,
        decay[None],
        skip,
        norm_gain[None],
        out_weight,
        residual,
        layer_gain[None],
        routes.T,
        route_weight.T,
        gate_up,
        gate_up_scale,
        down,
        down_scale,
    )
    return (stream.astype(jnp.float32) + mixed).astype(jnp.bfloat16)


def on_device(
    inputs,
    gating,
    write_proj,
    read_proj,
    step_raw,
    decay_log,
    skip_gain,
    norm_gain,
    out_weight,
    residual,
    routes,
    route_weight,
    layer_gain,
    gate_up_codes,
    gate_up_scales,
    down_codes,
    down_scales,
):
    return both_layers(
        inputs[0],
        gating[0],
        write_proj[0],
        read_proj[0],
        step_raw[0],
        decay_log,
        skip_gain,
        norm_gain,
        out_weight,
        residual[0],
        layer_gain,
        routes[0],
        route_weight[0],
        gate_up_codes[0],
        gate_up_scales[0],
        down_codes[0],
        down_scales[0],
    )[None]


def solution(mesh):
    placed = (
        P("seq", "ctx", "tp"),
        P("seq", "ctx", "tp"),
        P("seq", "ctx", "tp", None),
        P("seq", "ctx", "tp", None),
        P("seq", "ctx", "tp"),
        P("tp"),
        P("tp"),
        P("tp"),
        P("tp", "ctx"),
        P("seq", "ctx", "tp"),
        P("seq", "ctx", None),
        P("seq", "ctx", None),
        P("tp"),
        P(("ctx", "seq"), None, "tp", None),
        P(("ctx", "seq"), None, "tp", None),
        P(("ctx", "seq"), None, "tp"),
        P(("ctx", "seq"), None, "tp"),
    )
    return jax.shard_map(
        on_device, mesh=mesh, in_specs=placed, out_specs=P("seq", "ctx", "tp"), check_vma=False
    )
```

```python
import functools

import jax
import jax.numpy as jnp
from jax import lax
from jax.experimental import pallas as pl
from jax.experimental.pallas import tpu as pltpu
from jax.sharding import PartitionSpec as P

MESH = pl.DeviceIdType.MESH

QB = 128


EPSILON = 1e-05


def flip(index, offset, size):
    total, bit = 0, 1
    while bit < size:
        total = total + bit * ((index // bit + offset // bit) % 2)
        bit *= 2
    return total


def layer_kernel(
    sizes,
    value_ref,
    gating_ref,
    write_ref,
    read_ref,
    step_ref,
    decay_ref,
    skip_ref,
    norm_gain_ref,
    out_weight_hbm,
    residual_ref,
    layer_gain_ref,
    routes_ref,
    route_weight_ref,
    gate_up_hbm,
    gate_up_scale_ref,
    down_hbm,
    down_scale_ref,
    stream_ref,
    mixed_ref,
    out_weight_ref,
    gate_up_ref,
    down_ref,
    fetch_sem,
    contrib,
    state_in,
    state_out,
    rows_in,
    product,
    mixed_out,
    mixed_in,
    square_out,
    square_in,
    state_send,
    state_recv,
    rows_send,
    rows_recv,
    mixed_send,
    mixed_recv,
    square_send,
    square_recv,
    high_slots,
    low_slots,
    high_rows,
    low_rows,
    slots,
    w_gate_up,
    w_down,
    received,
    partial_out,
    partial_in,
    hidden,
    answers,
    returned,
    row_send,
    row_recv,
    part_send,
    part_recv,
    hid_send,
    hid_recv,
    ans_send,
    ans_recv,
    half_in,
    half_recv,
):
    n_ctx, n_seq, n_tp = sizes
    ctx, seq, tp = lax.axis_index("ctx"), lax.axis_index("seq"), lax.axis_index("tp")
    tokens, channels = value_ref.shape
    heads = step_ref.shape[0]
    groups, span = rows_in.shape[0], rows_in.shape[3]
    head_width = channels // heads
    per_group = heads // groups
    state_width = write_ref.shape[1] // groups
    columns, features = out_weight_ref.shape[1], residual_ref.shape[1]
    owners = features // columns
    pair = 2 * head_width
    f32, bf16 = jnp.float32, jnp.bfloat16

    def state_copy(g, target):
        return pltpu.make_async_remote_copy(
            src_ref=state_out.at[g],
            dst_ref=state_in.at[g],
            send_sem=state_send.at[g],
            recv_sem=state_recv.at[g],
            device_id={"ctx": target},
            device_id_type=MESH,
        )

    def rows_copy(g, source, slot, offset):
        return pltpu.make_async_remote_copy(
            src_ref=rows_in.at[g, source],
            dst_ref=rows_in.at[g, slot],
            send_sem=rows_send.at[g * n_ctx + slot],
            recv_sem=rows_recv.at[g * n_ctx + slot],
            device_id={"ctx": flip(ctx, offset, n_ctx)},
            device_id_type=MESH,
        )

    target_tp = ctx // owners

    def mixed_copy(a, slot):
        return pltpu.make_async_remote_copy(
            src_ref=mixed_out.at[a],
            dst_ref=mixed_in.at[slot],
            send_sem=mixed_send.at[a],
            recv_sem=mixed_recv.at[slot],
            device_id={"ctx": flip(ctx, a, n_ctx), "tp": target_tp},
            device_id_type=MESH,
        )

    def square_copy(i):
        return pltpu.make_async_remote_copy(
            src_ref=square_out,
            dst_ref=square_in.at[i - 1],
            send_sem=square_send.at[i - 1],
            recv_sem=square_recv.at[i - 1],
            device_id={"tp": lax.rem(tp + i, n_tp)},
            device_id_type=MESH,
        )

    barrier = pltpu.get_barrier_semaphore()
    for a in range(n_ctx):
        for i in range(n_tp):
            if a + i > 0:
                pl.semaphore_signal(
                    barrier,
                    inc=1,
                    device_id={"ctx": flip(ctx, a, n_ctx), "tp": lax.rem(tp + i, n_tp)},
                    device_id_type=MESH,
                )

    @pl.loop(n_ctx, n_ctx * n_seq)
    def _(r):
        pl.semaphore_signal(
            barrier,
            inc=1,
            device_id={"ctx": flip(ctx, r % n_ctx, n_ctx), "seq": flip(seq, r // n_ctx, n_seq)},
            device_id_type=MESH,
        )

    fetches = [
        pltpu.make_async_copy(source, target, fetch_sem.at[k])
        for k, (source, target) in enumerate(
            ((out_weight_hbm, out_weight_ref), (gate_up_hbm, gate_up_ref), (down_hbm, down_ref))
        )
    ]
    for fetch in fetches:
        fetch.start()

    step = step_ref[...]
    stride_t = jnp.maximum(step, 0.0) + jnp.log1p(jnp.exp(-jnp.abs(step)))
    stride = stride_t.T
    at_row = lax.broadcasted_iota(jnp.int32, (tokens, tokens), 0)
    at_col = lax.broadcasted_iota(jnp.int32, (tokens, tokens), 1)
    causal = at_row >= at_col
    cumul = jnp.dot(
        causal.astype(f32), stride * -jnp.exp(decay_ref[...]), precision=lax.Precision.HIGHEST
    )
    cumul_t = cumul.T
    final = cumul[tokens - 1 : tokens, :]
    coefficient = jnp.exp(final - cumul) * stride
    keep = jnp.exp(final)
    growth = jnp.exp(cumul)
    first_half = lax.broadcasted_iota(jnp.int32, (tokens, pair), 1) < head_width

    def widen(table, g):
        return jnp.concatenate(
            [
                jnp.where(first_half, table[:, h : h + 1], table[:, h + 1 : h + 2])
                for h in range(g * per_group, (g + 1) * per_group, 2)
            ],
            axis=1,
        )

    for g in range(groups):
        lanes = slice(g * span, (g + 1) * span)
        weighted = (value_ref[:, lanes].astype(f32) * widen(coefficient, g)).astype(bf16)
        contrib[g] = lax.dot_general(
            weighted,
            write_ref[:, g * state_width : (g + 1) * state_width],
            (((0,), (0,)), ((), ())),
            preferred_element_type=f32,
        )

    pl.semaphore_wait(barrier, n_ctx * (n_tp + n_seq - 1) - 1)

    @pl.when(ctx == 0)
    def _():
        state_in[...] = jnp.zeros_like(state_in)

    for g in range(groups):
        lanes = slice(g * span, (g + 1) * span)
        narrow = slice(g * state_width, (g + 1) * state_width)
        values = value_ref[:, lanes]
        scores = lax.dot_general(
            read_ref[:, narrow],
            write_ref[:, narrow],
            (((1,), (1,)), ((), ())),
            preferred_element_type=f32,
        )
        local = []
        for k in range(per_group // 2):
            block = values[:, k * pair : (k + 1) * pair]
            mixing = []
            for h in (g * per_group + 2 * k, g * per_group + 2 * k + 1):
                spread = cumul[:, h : h + 1] - cumul_t[h : h + 1, :]
                decay = jnp.exp(jnp.where(causal, spread, -jnp.inf)) * stride_t[h : h + 1, :]
                mixing.append((scores * decay).astype(bf16))
            zero = jnp.zeros_like(block)
            local.append(
                jnp.dot(
                    jnp.concatenate(mixing, axis=1),
                    jnp.concatenate(
                        [jnp.where(first_half, block, zero), jnp.where(first_half, zero, block)],
                        axis=0,
                    ),
                    preferred_element_type=f32,
                )
            )

        @pl.when(ctx > 0)
        def _():
            state_copy(g, ctx - 1).wait_recv()

        @pl.when(ctx < n_ctx - 1)
        def _():
            for j in range(per_group):
                h = g * per_group + j
                part = slice(j * head_width, (j + 1) * head_width)
                state_out[g, part, :] = (
                    state_in[g, part, :].astype(f32) * keep[:, h : h + 1] + contrib[g, part, :]
                ).astype(bf16)
            state_copy(g, ctx + 1).start()

        carried = lax.dot_general(
            read_ref[:, narrow],
            state_in[g],
            (((1,), (1,)), ((), ())),
            preferred_element_type=f32,
        )
        skip = jnp.concatenate(
            [
                jnp.where(first_half, skip_ref[h], skip_ref[h + 1])
                for h in range(g * per_group, (g + 1) * per_group, 2)
            ],
            axis=1,
        )
        output = (
            jnp.concatenate(local, axis=1)
            + widen(growth, g) * carried
            + skip * values.astype(f32)
        )
        gate = gating_ref[:, lanes].astype(f32)
        gated = output * (gate / (1.0 + jnp.exp(-gate)))
        scale = lax.rsqrt(jnp.mean(gated * gated, axis=1, keepdims=True) + EPSILON)
        rows_in[g, 0] = (gated * scale * norm_gain_ref[:, lanes]).astype(bf16)
        for a in range(2, n_ctx, 2):
            rows_copy(g, 0, a, a).start()
        rows_copy(g, 0, 1, 1).start()

    experts, capacity, feature_width = slots.shape
    half_width = w_down.shape[0]
    sources = n_ctx * n_seq
    ticks = lax.broadcasted_iota(jnp.int32, (experts, tokens), 0)
    named = [(ticks == routes_ref[k : k + 1, :]).astype(f32) for k in range(2)]
    earlier = jnp.dot(
        (named[0] + named[1]).astype(bf16),
        (at_row < at_col).astype(bf16),
        preferred_element_type=f32,
    )
    place = lax.broadcasted_iota(jnp.int32, (experts * capacity, tokens), 0)
    picker = jnp.zeros((experts * capacity, tokens), f32)
    weights = jnp.zeros((experts * capacity, tokens), f32)
    for k in range(2):
        rank = jnp.sum(named[k] * earlier, axis=0, keepdims=True).astype(jnp.int32)
        hit = place == routes_ref[k : k + 1, :] * capacity + rank
        picker = jnp.where(hit, 1.0, picker)
        weights = jnp.where(hit, route_weight_ref[k : k + 1, :], weights)
    picker = picker.astype(bf16)
    high = weights.astype(bf16)
    low = (weights - high.astype(f32)).astype(bf16)
    high_slots[...] = high.reshape(experts, capacity, tokens)
    low_slots[...] = low.reshape(experts, capacity, tokens)

    @pl.loop(0, experts)
    def _(q):
        holder = flip(ctx, q % n_ctx, n_ctx) * n_seq + flip(seq, q // n_ctx * 2, n_seq)
        high_rows[q] = high_slots[holder // 2]
        low_rows[q] = low_slots[holder // 2]

    for fetch in fetches:
        fetch.wait()

    def scale_gate_up(i):
        rows = slice(i * QB, (i + 1) * QB)
        for kind in range(2):
            for j in range(half_width // QB):
                lanes = slice(j * QB, (j + 1) * QB)
                target = slice(kind * half_width + j * QB, kind * half_width + (j + 1) * QB)
                w_gate_up[rows, target] = (
                    gate_up_ref[kind, rows, lanes].astype(f32)
                    * gate_up_scale_ref[j, kind : kind + 1, i : i + 1]
                ).astype(bf16)

    def scale_down(i):
        rows = slice(i * QB, (i + 1) * QB)
        for j in range(feature_width // QB):
            lanes = slice(j * QB, (j + 1) * QB)
            w_down[rows, lanes] = (
                down_ref[rows, lanes].astype(f32) * down_scale_ref[i, :, j : j + 1]
            ).astype(bf16)

    chores = [functools.partial(scale_gate_up, i) for i in range(feature_width // QB)]
    chores += [functools.partial(scale_down, i) for i in range(half_width // QB)]

    def multiply(g):
        for a in range(1, n_ctx, 2):
            rows_copy(g, 0, a, a).wait_recv()
        part = jnp.dot(
            rows_in[g].reshape(n_ctx * tokens, span),
            out_weight_ref[g * span : (g + 1) * span, :],
            preferred_element_type=f32,
        )
        if g > 0:
            part = part + product[...]
        if g < groups - 1:
            product[...] = part
        else:
            mixed_out[...] = part.astype(bf16).reshape(n_ctx, tokens, columns)

    for g in range(groups):
        for a in range(2, n_ctx, 2):
            rows_copy(g, 0, a, a).wait_recv()
            rows_copy(g, a, a + 1, 1).start()
        for chore in chores[g::groups]:
            chore()
        if g > 0:
            multiply(g - 1)
    multiply(groups - 1)

    own_slot = lax.rem(ctx, owners) * n_tp + tp
    for a in range(1, n_ctx):
        mixed_copy(a, own_slot).start()

    @pl.when(tp == target_tp)
    def _():
        mixed_in[own_slot] = mixed_out[0]

    @pl.when(tp != target_tp)
    def _():
        mixed_copy(0, own_slot).start()

    squares = jnp.zeros((tokens, 1), f32)
    for q in range(owners):
        lanes = slice(q * columns, (q + 1) * columns)
        total = residual_ref[:, lanes].astype(f32)
        for i in range(n_tp):

            @pl.when((ctx != tp * owners + q) | (tp != i))
            def _():
                mixed_copy(1, q * n_tp + i).wait_recv()

            total = total + mixed_in[q * n_tp + i].astype(f32)
        total = total.astype(bf16)
        stream_ref[:, lanes] = total
        total = total.astype(f32)
        squares = squares + jnp.sum(total * total, axis=1, keepdims=True)
    across = jnp.broadcast_to(squares, (tokens, tokens)).T[:8]
    square_out[...] = across
    for i in range(1, n_tp):
        square_copy(i).start()
    for i in range(1, n_tp):
        square_copy(i).wait_recv()
        across = across + square_in[i - 1]
    squares = jnp.broadcast_to(across[:1], (tokens, tokens)).T[:, :1]
    scale = lax.rsqrt(squares / (features * n_tp) + EPSILON)
    expert_in = (stream_ref[...].astype(f32) * scale * layer_gain_ref[...]).astype(bf16)
    slots[...] = (
        jnp.dot(picker, expert_in, preferred_element_type=f32)
        .astype(bf16)
        .reshape(experts, capacity, feature_width)
    )

    teams = sources // n_tp

    def at_offset(r):
        return flip(ctx, r % n_ctx, n_ctx), flip(seq, r // n_ctx, n_seq)

    def row_copy(r):
        c, s = at_offset(r)
        return pltpu.make_async_remote_copy(
            src_ref=slots.at[(c * n_seq + s) // 2],
            dst_ref=received.at[r],
            send_sem=row_send.at[r],
            recv_sem=row_recv.at[r],
            device_id={"ctx": c, "seq": s},
            device_id_type=MESH,
        )

    def part_copy(g, i):
        peer = lax.rem(tp + i, n_tp)
        return pltpu.make_async_remote_copy(
            src_ref=partial_out.at[g * n_tp + peer],
            dst_ref=partial_in.at[g * (n_tp - 1) + i - 1],
            send_sem=part_send.at[g * (n_tp - 1) + i - 1],
            recv_sem=part_recv.at[g * (n_tp - 1) + i - 1],
            device_id={"tp": peer},
            device_id_type=MESH,
        )

    def hid_copy(g, i):
        peer = lax.rem(tp + i, n_tp)
        return pltpu.make_async_remote_copy(
            src_ref=hidden.at[g * n_tp + tp],
            dst_ref=hidden.at[g * n_tp + tp],
            send_sem=hid_send.at[g * (n_tp - 1) + i - 1],
            recv_sem=hid_recv.at[g * (n_tp - 1) + i - 1],
            device_id={"tp": peer},
            device_id_type=MESH,
        )

    def hid_arrival(g, i):
        origin = lax.rem(tp + n_tp - i, n_tp)
        return pltpu.make_async_remote_copy(
            src_ref=hidden.at[g * n_tp + origin],
            dst_ref=hidden.at[g * n_tp + origin],
            send_sem=hid_send.at[g * (n_tp - 1) + i - 1],
            recv_sem=hid_recv.at[g * (n_tp - 1) + i - 1],
            device_id={"tp": origin},
            device_id_type=MESH,
        )

    def near(r):
        return (r // n_ctx) % 2 == 0

    def slot(r):
        return r // (2 * n_ctx) * n_ctx + r % n_ctx

    def forward_copy(r):
        return pltpu.make_async_remote_copy(
            src_ref=received.at[r],
            dst_ref=received.at[r + n_ctx],
            send_sem=row_send.at[r + n_ctx],
            recv_sem=row_recv.at[r + n_ctx],
            device_id={"seq": flip(seq, 1, n_seq)},
            device_id_type=MESH,
        )

    def half_copy(r):
        return pltpu.make_async_remote_copy(
            src_ref=answers.at[r],
            dst_ref=half_in.at[slot(r - n_ctx)],
            send_sem=ans_send.at[r],
            recv_sem=half_recv.at[slot(r - n_ctx)],
            device_id={"seq": flip(seq, 1, n_seq)},
            device_id_type=MESH,
        )

    def ans_copy(r):
        c, s = at_offset(r)
        return pltpu.make_async_remote_copy(
            src_ref=answers.at[r],
            dst_ref=returned.at[slot(r)],
            send_sem=ans_send.at[r],
            recv_sem=ans_recv.at[slot(r)],
            device_id={"ctx": c, "seq": s},
            device_id_type=MESH,
        )

    @pl.loop(1, sources)
    def _(r):
        @pl.when(near(r))
        def _():
            row_copy(r).start()

    received[0] = slots[(ctx * n_seq + seq) // 2]
    forward_copy(0).start()

    delay = n_ctx // n_tp + 1

    @pl.loop(0, teams + 3)
    def _(step):
        @pl.when(step < teams)
        def _():
            g = step
            for i in range(n_tp):
                r = g * n_tp + i
                if i == 0:

                    @pl.when(g > 0)
                    def _():
                        row_copy(r).wait_recv()
                else:
                    row_copy(r).wait_recv()

                @pl.when(near(r) & (r > 0))
                def _():
                    forward_copy(r).start()
            rows = received[pl.ds(g * n_tp, n_tp)].reshape(n_tp * capacity, feature_width)
            both = jnp.dot(rows, w_gate_up[...], preferred_element_type=jnp.float32)
            partial_out[pl.ds(g * n_tp, n_tp)] = both.astype(jnp.bfloat16).reshape(
                n_tp, capacity, 2 * half_width
            )
            for i in range(1, n_tp):
                part_copy(g, i).start()

        @pl.when((step >= 1) & (step < teams + 1))
        def _():
            g = step - 1
            total = partial_out[g * n_tp + tp].astype(jnp.float32)
            for i in range(1, n_tp):
                part_copy(g, i).wait_recv()
                total = total + partial_in[g * (n_tp - 1) + i - 1].astype(jnp.float32)
            gate, up = total[:, :half_width], total[:, half_width:]
            hidden[g * n_tp + tp] = (gate / (1.0 + jnp.exp(-gate)) * up).astype(jnp.bfloat16)
            for i in range(1, n_tp):
                hid_copy(g, i).start()

        @pl.when((step >= 2) & (step < teams + 2))
        def _():
            g = step - 2
            for i in range(1, n_tp):
                hid_arrival(g, i).wait_recv()
            rows = hidden[pl.ds(g * n_tp, n_tp)].reshape(n_tp * capacity, half_width)
            answer = jnp.dot(rows, w_down[...], preferred_element_type=jnp.float32)
            answers[pl.ds(g * n_tp, n_tp)] = answer.astype(jnp.bfloat16).reshape(
                n_tp, capacity, feature_width
            )
            for i in range(n_tp):
                r = g * n_tp + i

                @pl.when((r // n_ctx) % 2 == 1)
                def _():
                    half_copy(r).start()

        @pl.when(step >= 2 + delay)
        def _():
            for i in range(n_tp):
                r = (step - 2 - delay) * n_tp + i

                @pl.when(near(r))
                def _():
                    half_copy(r + n_ctx).wait_recv()
                    answers[r] = (
                        answers[r].astype(jnp.float32) + half_in[slot(r)].astype(jnp.float32)
                    ).astype(jnp.bfloat16)

                    @pl.when(r > 0)
                    def _():
                        ans_copy(r).start()

    returned[0] = answers[0]

    @pl.loop(1, sources)
    def _(r):
        @pl.when(near(r))
        def _():
            ans_copy(r).wait_recv()

    back = returned[...].reshape(experts * capacity, feature_width)
    contract = (((0,), (0,)), ((), ()))
    mixed = 0.0
    for rows in (high_rows, low_rows):
        mixed = mixed + lax.dot_general(
            rows[...].reshape(experts * capacity, tokens),
            back,
            contract,
            preferred_element_type=f32,
        )
    mixed_ref[...] = mixed

    @pl.loop(1, sources)
    def _(r):
        row_copy(r).wait_send()
        pltpu.make_async_remote_copy(
            src_ref=answers.at[r],
            dst_ref=returned.at[0],
            send_sem=ans_send.at[r],
            recv_sem=ans_recv.at[0],
            device_id={"seq": flip(seq, 1, n_seq)},
            device_id_type=MESH,
        ).wait_send()

    @pl.loop(0, teams)
    def _(g):
        for i in range(1, n_tp):
            part_copy(g, i).wait_send()
            hid_copy(g, i).wait_send()

    for i in range(1, n_tp):
        square_copy(i).wait_send()
    for a in range(1, n_ctx):
        mixed_copy(a, own_slot).wait_send()

    @pl.when(tp != target_tp)
    def _():
        mixed_copy(0, own_slot).wait_send()

    for g in range(groups):
        for a in range(1, n_ctx):
            rows_copy(g, 0, a, a).wait_send()

    @pl.when(ctx < n_ctx - 1)
    def _():
        for g in range(groups):
            state_copy(g, ctx + 1).wait_send()


def both_layers(
    values,
    gating,
    writes,
    reads,
    step,
    decay,
    skip,
    norm_gain,
    out_weight,
    residual,
    layer_gain,
    routes,
    route_weight,
    gate_up,
    gate_up_scale,
    down,
    down_scale,
):
    sizes = tuple(lax.axis_size(axis) for axis in ("ctx", "seq", "tp"))
    n_ctx, n_seq, n_tp = sizes
    tokens, channels = values.shape
    groups, state_width = writes.shape[1], writes.shape[2]
    span = channels // groups
    columns, features = out_weight.shape[1], residual.shape[1]
    sources = n_ctx * n_seq
    experts = sources // 2
    capacity = -(-(3 * tokens // experts) // 16) * 16
    half_width = down.shape[0]
    shares = sources // n_tp * (n_tp - 1)
    slots = features // columns * n_tp
    dma = pltpu.SemaphoreType.DMA
    vmem, smem = pl.BlockSpec(memory_space=pltpu.VMEM), pl.BlockSpec(memory_space=pltpu.SMEM)
    hbm = pl.BlockSpec(memory_space=pl.ANY)

    def wide(*shape):
        return pltpu.VMEM(shape, jnp.float32)

    def half(*shape):
        return pltpu.VMEM(shape, jnp.bfloat16)

    stream, mixed = pl.pallas_call(
        functools.partial(layer_kernel, sizes),
        out_shape=(
            jax.ShapeDtypeStruct((tokens, features), jnp.bfloat16),
            jax.ShapeDtypeStruct((tokens, features), jnp.float32),
        ),
        in_specs=[vmem] * 6
        + [smem, vmem, hbm, vmem, vmem, vmem, vmem]
        + [hbm, vmem, hbm, vmem],
        out_specs=(vmem, vmem),
        scratch_shapes=[
            half(*out_weight.shape),
            half(*gate_up.shape),
            half(*down.shape),
            dma((3,)),
            wide(groups, span, state_width),
            half(groups, span, state_width),
            half(groups, span, state_width),
            half(groups, n_ctx, tokens, span),
            wide(n_ctx * tokens, columns),
            half(n_ctx, tokens, columns),
            half(slots, tokens, columns),
            wide(8, tokens),
            wide(n_tp - 1, 8, tokens),
            dma((groups,)),
            dma((groups,)),
            dma((groups * n_ctx,)),
            dma((groups * n_ctx,)),
            dma((n_ctx,)),
            dma((slots,)),
            dma((n_tp - 1,)),
            dma((n_tp - 1,)),
            half(experts, capacity, tokens),
            half(experts, capacity, tokens),
            half(experts, capacity, tokens),
            half(experts, capacity, tokens),
            half(experts, capacity, features),
            half(features, 2 * half_width),
            half(half_width, features),
            half(sources, capacity, features),
            half(sources, capacity, 2 * half_width),
            half(shares, capacity, 2 * half_width),
            half(sources, capacity, half_width),
            half(sources, capacity, features),
            half(experts, capacity, features),
            dma((sources,)),
            dma((sources,)),
            dma((shares,)),
            dma((shares,)),
            dma((shares,)),
            dma((shares,)),
            dma((sources,)),
            dma((experts,)),
            half(experts, capacity, features),
            dma((experts,)),
        ],
        compiler_params=pltpu.CompilerParams(
            collective_id=1, has_side_effects=True, vmem_limit_bytes=60 * 1024 * 1024
        ),
    )(
        values,
        gating,
        writes.reshape(tokens, groups * state_width),
        reads.reshape(tokens, groups * state_width),
        step.T,
        decay[None],
        skip,
        norm_gain[None],
        out_weight,
        residual,
        layer_gain[None],
        routes.T,
        route_weight.T,
        gate_up,
        jnp.transpose(gate_up_scale, (2, 0, 1)),
        down,
        down_scale[:, None, :],
    )
    return (stream.astype(jnp.float32) + mixed).astype(jnp.bfloat16)


def on_device(
    inputs,
    gating,
    write_proj,
    read_proj,
    step_raw,
    decay_log,
    skip_gain,
    norm_gain,
    out_weight,
    residual,
    routes,
    route_weight,
    layer_gain,
    gate_up_codes,
    gate_up_scales,
    down_codes,
    down_scales,
):
    return both_layers(
        inputs[0],
        gating[0],
        write_proj[0],
        read_proj[0],
        step_raw[0],
        decay_log,
        skip_gain,
        norm_gain,
        out_weight,
        residual[0],
        layer_gain,
        routes[0],
        route_weight[0],
        gate_up_codes[0],
        gate_up_scales[0],
        down_codes[0],
        down_scales[0],
    )[None]


def solution(mesh):
    placed = (
        P("seq", "ctx", "tp"),
        P("seq", "ctx", "tp"),
        P("seq", "ctx", "tp", None),
        P("seq", "ctx", "tp", None),
        P("seq", "ctx", "tp"),
        P("tp"),
        P("tp"),
        P("tp"),
        P("tp", "ctx"),
        P("seq", "ctx", "tp"),
        P("seq", "ctx", None),
        P("seq", "ctx", None),
        P("tp"),
        P(("ctx", "seq"), None, "tp", None),
        P(("ctx", "seq"), None, "tp", None),
        P(("ctx", "seq"), None, "tp"),
        P(("ctx", "seq"), None, "tp"),
    )
    return jax.shard_map(
        on_device, mesh=mesh, in_specs=placed, out_specs=P("seq", "ctx", "tp"), check_vma=False
    )
```
